256 devices in a mesh: row: 32 (over y, z), col: 8 (over x, core).
Axes of the slice: x: 4, y: 4, z: 8, core: 2. Of those that a mesh axis runs over, the one named last changes fastest.
Arguments:
- tail_factor: bfloat16 [131072, 1024], P('row'), may hold values from -0.015625 to 0.015625
- tail_solution: bfloat16 [131072, 2048], P('row', 'col'), may hold values from -6 to 6
- panel_rhs: float32 [1024, 2048], P('row', 'col'), may hold values from -6 to 6
- panel_factor: bfloat16 [3, 512, 512], P(None, 'col'), as said below
Outputs:
- panel_solution: float32 [1024, 2048], P(None, 'col')
The draws below stay inside these ranges and needn't reach their ends.
Inputs may be any that keep to these rules, and one draw needn't show every extreme that they name: panel_factor[0] and panel_factor[1] are unit lower triangular: ones on the diagonal and zeros above it.
All inputs are finite; a program needn't handle non-finite values.
Results may differ from the reference program's by a relative error of at most 0.0003.
Values may be sent and summed in bfloat16 or wider, within the bound.
A program may use at most 64 MiB of HBM per device.

```python
import math
import jax
import jax.numpy as jnp
from jax import lax

BLOCK = 512
TAIL = 131072
RHS = 2048


def draw_panel_factor(key, part):
    subkey = jax.random.fold_in(key, 11)
    values = jax.random.normal(subkey, (3, BLOCK, BLOCK), jnp.float32)
    row_index = lax.broadcasted_iota(jnp.int32, (BLOCK, BLOCK), 0)
    col_index = lax.broadcasted_iota(jnp.int32, (BLOCK, BLOCK), 1)
    strict = (row_index > col_index).astype(jnp.float32)
    identity = (row_index == col_index).astype(jnp.float32)
    diagonal_part = values[:2] * (0.35 / math.sqrt(BLOCK)) * strict + identity
    coupling = values[2:] * (0.7 / math.sqrt(BLOCK))
    return jnp.concatenate([diagonal_part, coupling], axis=0).astype(jnp.bfloat16)


def block_scale(rng, shape, shards, low, high):
    level = 1.0
    for dim, blocks in shards:
        draws = jax.random.uniform(jax.random.fold_in(jax.random.fold_in(rng, 6), dim), (blocks,), jnp.float32, low / len(shards), high / len(shards))
        level = level * jnp.repeat(jnp.exp(draws), shape[dim] // blocks).reshape((-1,) + (1,) * (len(shape) - 1 - dim))
    return level


def centred(key, extent, scale, reach, pieces=(), held_as=jnp.bfloat16):
    entries = scale * jax.random.normal(key, extent, jnp.float32)
    if pieces:
        entries = entries * block_scale(key, extent, pieces, -0.22, 0.18)
    return jnp.clip(entries, -reach, reach).astype(held_as)


def setup_inputs(seed: int = 0) -> dict:
    streams_of = jax.random.split(jax.random.key(seed), 5)
    tail_factor = centred(streams_of[0], (TAIL, 2 * BLOCK), TAIL ** -0.5, 0.015625, ((0, 32),))
    tail_solution = centred(streams_of[1], (TAIL, RHS), 1.0, 6.0, ((0, 32), (1, 8)))
    panel_rhs = centred(streams_of[2], (2 * BLOCK, RHS), 1.0, 6.0, ((0, 32), (1, 8)), jnp.float32)
    panel_factor = draw_panel_factor(jax.random.fold_in(streams_of[4], 71), 0)
    return dict(tail_factor=tail_factor, tail_solution=tail_solution, panel_rhs=panel_rhs, panel_factor=panel_factor)


def solve_block(lower, rhs):
    return jax.scipy.linalg.solve_triangular(lower, rhs, trans=1, lower=True, unit_diagonal=True)

def reference(tail_factor, tail_solution, panel_rhs, panel_factor):
    update = lax.dot_general(tail_factor.astype(jnp.float32), tail_solution.astype(jnp.float32), (((0,), (0,)), ((), ())), preferred_element_type=jnp.float32)
    reduced = panel_rhs - update
    blocks = panel_factor.astype(jnp.float32)
    solution_second = solve_block(blocks[1], reduced[BLOCK:])
    adjusted = reduced[:BLOCK] - jnp.dot(blocks[2].T.astype(jnp.float32), solution_second.astype(jnp.float32), precision=lax.Precision.HIGHEST, preferred_element_type=jnp.float32)
    solution_first = solve_block(blocks[0], adjusted)
    return jnp.concatenate([solution_first, solution_second], axis=0)
```

```python
import jax
import jax.numpy as jnp
from jax import lax
from jax.experimental import pallas as pl
from jax.experimental.pallas import tpu as pltpu
from jax.sharding import PartitionSpec as P

MESH = pl.DeviceIdType.MESH
F32 = jnp.float32
BF16 = jnp.bfloat16

NY, NZ, NX = 4, 8, 4
BLOCK = 512
WINDOW = 2 * BLOCK
PIECE = 256
PIECES = WINDOW // PIECE
SUB = 128
SUBS = BLOCK // SUB


def split(x):
    high = x.astype(BF16)
    return high, (x - high.astype(F32)).astype(BF16)


def mm(a, b):
    return jnp.dot(a, b, preferred_element_type=F32)


def mm_exact(a, b):
    high, low = split(a)
    return mm(high, b) + mm(low, b)


def mm_split(a, b):
    a_high, a_low = split(a)
    b_high, b_low = split(b)
    return mm(a_high, b_high) + (mm(a_low, b_high) + mm(a_high, b_low))


def unit_inverse(lower):
    row = lax.broadcasted_iota(jnp.int32, (SUB, SUB), 0)
    col = lax.broadcasted_iota(jnp.int32, (SUB, SUB), 1)
    block = lower.astype(F32)

    def below(size):
        inside = (row // (2 * size) == col // (2 * size)) & (row // size == col // size + 1)
        return jnp.where(inside, block, 0.0)

    inverse = jnp.where(row == col, 1.0, 0.0) - below(1)
    size = 2
    while size < SUB:
        inverse = inverse - mm_split(mm_exact(inverse, below(size).astype(BF16)), inverse)
        size *= 2
    return inverse


def kernel(
    a_hbm, b_hbm, rhs_hbm, panel_hbm, out_ref,
    a_v, b_v, bt, rhs_v, place, ut, yrecv, w, zrecv, g, lf, blk, dinv, mh, ml,
    load_sem, y_s, y_r, z_s, z_r, gz_s, gz_r, gy_s, gy_r,
    px_s, px_r, pc_s, pc_r, dx_s, dx_r, dc_s, dc_r,
):
    row, col = lax.axis_index("row"), lax.axis_index("col")
    y, z = row // NZ, row % NZ
    x, core = col // 2, col % 2
    other = x * 2 + (1 - core)
    right = lax.rem(y + 1, NY) * NZ + z
    left = lax.rem(y + NY - 1, NY) * NZ + z
    depth = a_hbm.shape[0]
    width = b_hbm.shape[1]
    group = width // NY
    half = group // 2
    own = width // (NY * NZ)

    def remote(src, dst, send, recv, r, c):
        return pltpu.make_async_remote_copy(
            src_ref=src, dst_ref=dst, send_sem=send, recv_sem=recv,
            device_id=(r, c), device_id_type=MESH,
        )

    def z_peer(d):
        return y * NZ + lax.rem(z + d, NZ)

    def x_peer(d):
        return lax.rem(x + d, NX) * 2 + core

    loads = [pltpu.make_async_copy(b_hbm, b_v, load_sem.at[0])]
    for n in range(PIECES - 1, -1, -1):
        loads.append(
            pltpu.make_async_copy(a_hbm.at[:, PIECE * n : PIECE * (n + 1)], a_v.at[n], load_sem.at[1 + n])
        )
    loads.append(pltpu.make_async_copy(rhs_hbm, rhs_v, load_sem.at[5]))
    loads.append(pltpu.make_async_copy(panel_hbm, lf.at[:, col], load_sem.at[6]))
    for load in loads:
        load.start()

    barrier = pltpu.get_barrier_semaphore()

    def greet(r, c):
        pl.semaphore_signal(barrier, inc=1, device_id=(r, c), device_id_type=MESH)

    greet(left, col)
    greet(right, col)
    for d in range(1, NZ):
        greet(z_peer(d), col)
    for d in range(1, NX):
        greet(row, x_peer(d))
    greet(row, other)

    place[...] = jnp.zeros_like(place)
    loads[5].wait()
    place[pl.ds(pl.multiple_of(z * 32, 8), 32), :] = rhs_v[...]
    loads[0].wait()
    for k in range(0, depth, 512):
        bt[:, k : k + 512] = b_v[k : k + 512, :].T

    pl.semaphore_wait(barrier, 2 + (NZ - 1) + (NX - 1) + 1)

    for d in range(1, NX):
        remote(panel_hbm, lf.at[:, col], px_s.at[d - 1], px_r.at[d - 1], row, x_peer(d)).start()
    remote(panel_hbm, lf.at[:, col], pc_s.at[0], pc_r.at[0], row, other).start()

    def y_group(target):
        return pl.multiple_of(target // NZ * group, group)

    right_rows, left_rows = y_group(right), y_group(left)
    far_rows = pl.multiple_of(lax.rem(y + 2, NY) * group, group)
    own_rows = pl.multiple_of(y * group, group)

    def y_copy(n, slot):
        start = ((right_rows, 1), (far_rows, 0), (right_rows, 0), (left_rows, 0), (far_rows, 1), (left_rows, 1))[slot]
        src = ut.at[n, pl.ds(start[0] + start[1] * half, half), :]
        target = right if slot < 3 else left
        return remote(src, yrecv.at[n, slot], y_s.at[n, slot], y_r.at[n, slot], target, col)

    def update(step, carry):
        n = PIECES - 1 - step
        pltpu.make_async_copy(a_hbm.at[:, 0:PIECE], a_v.at[n], load_sem.at[1 + n]).wait()
        ut[n] = mm(bt[...], a_v[n])

        @pl.when(n == y)
        def _():
            ut[n] = ut[n] - place[...].T

        for slot in (1, 4, 0, 3):
            y_copy(n, slot).start()
        return carry

    lax.fori_loop(0, PIECES, update, 0)

    def relay(n):
        y_copy(n, 1).wait_recv()
        ut[n, pl.ds(right_rows, half), :] += yrecv[n, 1]
        y_copy(n, 2).start()
        y_copy(n, 4).wait_recv()
        ut[n, pl.ds(left_rows + half, half), :] += yrecv[n, 4]
        y_copy(n, 5).start()

    def y_sum(n):
        for slot in (0, 2, 3, 5):
            y_copy(n, slot).wait_recv()
        columns = slice(n % 2 * PIECE, (n % 2 + 1) * PIECE)
        w[n // 2, :half, columns] = ut[n, pl.ds(own_rows, half), :] + (yrecv[n, 2] + yrecv[n, 3])
        w[n // 2, half:, columns] = ut[n, pl.ds(own_rows + half, half), :] + (yrecv[n, 0] + yrecv[n, 5])

    def z_copies(h):
        copies = []
        for d in range(1, NZ):
            target = z_peer(d)
            start = pl.multiple_of(lax.rem(z + d, NZ) * own, own)
            copies.append(
                remote(w.at[h, pl.ds(start, own), :], zrecv.at[h, d - 1], z_s.at[h, d - 1], z_r.at[h, d - 1], target, col)
            )
        return copies

    relay(3)
    relay(2)

    loads[6].wait()
    remote(panel_hbm, lf.at[:, col], pc_s.at[0], pc_r.at[0], row, other).wait_recv()
    at = pl.multiple_of(x * SUB, SUB)
    blk[...] = jnp.concatenate(
        [lf[core, 2 * x, :, pl.ds(at, SUB)], lf[core, 2 * x + 1, :, pl.ds(at, SUB)]], axis=0
    )
    dinv[core, x] = unit_inverse(blk[...])
    mine = dinv.at[core, x]
    for d in range(1, NX):
        remote(mine, mine, dx_s.at[d - 1], dx_r.at[d - 1], row, x_peer(d)).start()
    remote(mine, mine, dc_s.at[0], dc_r.at[0], row, other).start()

    relay(1)
    relay(0)
    for h in (1, 0):
        y_sum(2 * h + 1)
        y_sum(2 * h)
        for copy in z_copies(h):
            copy.start()

    def forward_panel(d):
        shard = lf.at[:, lax.rem(x + NX - d, NX) * 2 + core]
        return remote(shard, shard, pc_s.at[d], pc_r.at[d], row, other)

    def forward_inverse(d):
        inverse = dinv.at[core, lax.rem(x + NX - d, NX)]
        return remote(inverse, inverse, dc_s.at[d], dc_r.at[d], row, other)

    for d in range(1, NX):
        remote(panel_hbm, lf.at[:, col], px_s.at[d - 1], px_r.at[d - 1], row, x_peer(d)).wait_recv()
        forward_panel(d).start()
    for d in range(1, NX):
        remote(mine, mine, dx_s.at[d - 1], dx_r.at[d - 1], row, x_peer(d)).wait_recv()
        forward_inverse(d).start()
    remote(mine, mine, dc_s.at[0], dc_r.at[0], row, other).wait_recv()
    for d in range(1, NX):
        forward_panel(d).wait_recv()
        forward_inverse(d).wait_recv()

    def whole_inverse(m):
        def lower(i, j):
            block = lf[m, :, :, SUB * j : SUB * (j + 1)].reshape(BLOCK, SUB)
            return block[SUB * i : SUB * (i + 1)]

        def pair(i):
            first, second = dinv[m, i], dinv[m, i + 1]
            below = -mm_split(mm_exact(second, lower(i + 1, i)), first)
            top = jnp.concatenate([first, jnp.zeros_like(first)], axis=1)
            return jnp.concatenate([top, jnp.concatenate([below, second], axis=1)], axis=0)

        first, second = pair(0), pair(2)
        off = lf[m, :, :, : 2 * SUB].reshape(BLOCK, 2 * SUB)[2 * SUB :]
        below = -mm_split(mm_exact(second, off), first)
        for rows, columns, value in (
            (slice(0, 2 * SUB), slice(0, 2 * SUB), first),
            (slice(0, 2 * SUB), slice(2 * SUB, BLOCK), jnp.zeros_like(first)),
            (slice(2 * SUB, BLOCK), slice(0, 2 * SUB), below),
            (slice(2 * SUB, BLOCK), slice(2 * SUB, BLOCK), second),
        ):
            high, low = split(value)
            mh[m, rows, columns] = high
            ml[m, rows, columns] = low

    whole_inverse(1)
    whole_inverse(0)

    def reduced(h):
        for copy in z_copies(h):
            copy.wait_recv()
        total = w[h, pl.ds(pl.multiple_of(z * own, own), own), :]
        for d in range(1, NZ):
            total = total + zrecv[h, d - 1]
        return -total

    def solve(h, value):
        high, low = split(value)
        return mm(high, mh[h]) + (mm(low, mh[h]) + mm(high, ml[h]))

    def gz_copies(h):
        mine_rows = g.at[h, pl.ds(pl.multiple_of(row * own, own), own), :]
        return [
            remote(mine_rows, mine_rows, gz_s.at[h, d - 1], gz_r.at[h, d - 1], z_peer(d), col)
            for d in range(1, NZ)
        ]

    def publish(h, value):
        g[h, pl.ds(pl.multiple_of(row * own, own), own), :] = value
        for copy in gz_copies(h):
            copy.start()

    second = solve(1, reduced(1))
    publish(1, second)
    coupling = lf[2].reshape(BLOCK, BLOCK)
    first = solve(0, reduced(0) - mm_exact(second, coupling))
    publish(0, first)

    def gy_copy(h, slot):
        start, size, target = (
            (own_rows, group, right), (own_rows, group, left),
            (left_rows, half, right), (right_rows + half, half, left),
        )[slot]
        rows = g.at[h, pl.ds(start, size), :]
        return remote(rows, rows, gy_s.at[h, slot], gy_r.at[h, slot], target, col)

    for h in (1, 0):
        for copy in gz_copies(h):
            copy.wait_recv()
        gy_copy(h, 0).start()
        gy_copy(h, 1).start()
    for h in (1, 0):
        gy_copy(h, 0).wait_recv()
        gy_copy(h, 2).start()
        gy_copy(h, 1).wait_recv()
        gy_copy(h, 3).start()
    for h in (1, 0):
        gy_copy(h, 2).wait_recv()
        gy_copy(h, 3).wait_recv()
        out_ref[h * BLOCK : (h + 1) * BLOCK, :] = g[h].T

    for n in range(PIECES):
        for slot in range(6):
            y_copy(n, slot).wait_send()
    for h in (1, 0):
        for copy in (*z_copies(h), *gz_copies(h)):
            copy.wait_send()
        for slot in range(4):
            gy_copy(h, slot).wait_send()
    for d in range(1, NX):
        remote(panel_hbm, lf.at[:, col], px_s.at[d - 1], px_r.at[d - 1], row, x_peer(d)).wait_send()
        remote(mine, mine, dx_s.at[d - 1], dx_r.at[d - 1], row, x_peer(d)).wait_send()
        forward_panel(d).wait_send()
        forward_inverse(d).wait_send()
    remote(panel_hbm, lf.at[:, col], pc_s.at[0], pc_r.at[0], row, other).wait_send()
    remote(mine, mine, dc_s.at[0], dc_r.at[0], row, other).wait_send()


def shards(tail_factor, tail_solution, panel_rhs, panel_factor):
    depth, window = tail_factor.shape
    width = tail_solution.shape[1]
    group, own = width // NY, width // (NY * NZ)
    slab = panel_factor.shape[1]
    dma = pltpu.SemaphoreType.DMA
    scratch = [
        pltpu.VMEM((PIECES, depth, PIECE), BF16),
        pltpu.VMEM((depth, width), BF16),
        pltpu.VMEM((width, depth), BF16),
        pltpu.VMEM(panel_rhs.shape, F32),
        pltpu.VMEM((PIECE, width), F32),
        pltpu.VMEM((PIECES, width, PIECE), F32),
        pltpu.VMEM((PIECES, 6, group // 2, PIECE), F32),
        pltpu.VMEM((2, group, BLOCK), F32),
        pltpu.VMEM((2, NZ - 1, own, BLOCK), F32),
        pltpu.VMEM((2, width, BLOCK), F32),
        pltpu.VMEM((3, 2 * NX, slab, BLOCK), BF16),
        pltpu.VMEM((SUB, SUB), BF16),
        pltpu.VMEM((2, SUBS, SUB, SUB), F32),
        pltpu.VMEM((2, BLOCK, BLOCK), BF16),
        pltpu.VMEM((2, BLOCK, BLOCK), BF16),
        dma((7,)),
        dma((PIECES, 6)), dma((PIECES, 6)),
        dma((2, NZ - 1)), dma((2, NZ - 1)),
        dma((2, NZ - 1)), dma((2, NZ - 1)),
        dma((2, 4)), dma((2, 4)),
        dma((NX - 1,)), dma((NX - 1,)),
        dma((NX,)), dma((NX,)),
        dma((NX - 1,)), dma((NX - 1,)),
        dma((NX,)), dma((NX,)),
    ]
    return pl.pallas_call(
        kernel,
        out_shape=jax.ShapeDtypeStruct((window, width), F32),
        in_specs=[pl.BlockSpec(memory_space=pl.ANY)] * 4,
        out_specs=pl.BlockSpec(memory_space=pltpu.VMEM),
        scratch_shapes=scratch,
        compiler_params=pltpu.CompilerParams(
            collective_id=0, has_side_effects=True, vmem_limit_bytes=60 * 1024 * 1024
        ),
    )(tail_factor, tail_solution, panel_rhs, panel_factor)


def solution(mesh):
    return jax.shard_map(
        shards,
        mesh=mesh,
        in_specs=(P("row", None), P("row", "col"), P("row", "col"), P(None, "col", None)),
        out_specs=P(None, "col"),
        check_vma=False,
    )
```

```python
import jax
import jax.numpy as jnp
from jax import lax
from jax.experimental import pallas as pl
from jax.experimental.pallas import tpu as pltpu
from jax.sharding import PartitionSpec as P

MESH = pl.DeviceIdType.MESH
F32 = jnp.float32
BF16 = jnp.bfloat16

NY, NZ, NX = 4, 8, 4
BLOCK = 512
WINDOW = 2 * BLOCK
PIECE = 256
PIECES = WINDOW // PIECE
SUB = 128
CHUNKS = 4
NEAR, FAR = (1, 7, 2, 6), (3, 5, 4)
Z_ORDER = (4, 3, 5, 2, 6, 1, 7)
Y_SLOT = (2, 0, 3, 4, 1, 5)
Y_SEM = (2, 0, 2, 2, 1, 2)
PARTS = 4


def split(x):
    high = x.astype(BF16)
    return high, (x - high.astype(F32)).astype(BF16)


def mm(a, b):
    return jnp.dot(a, b, preferred_element_type=F32)


def mm_exact(a, b):
    high, low = split(a)
    return mm(high, b) + mm(low, b)


def mm_split(a, b):
    a_high, a_low = split(a)
    b_high, b_low = split(b)
    return mm(a_high, b_high) + (mm(a_low, b_high) + mm(a_high, b_low))


def stacked(a, b):
    rows = a.shape[0]
    both = mm(jnp.concatenate(split(a), axis=0), b)
    return both[:rows] + both[rows:]


def within(size):
    row = lax.broadcasted_iota(jnp.int32, (SUB, SUB), 0)
    col = lax.broadcasted_iota(jnp.int32, (SUB, SUB), 1)
    return (row // (2 * size) == col // (2 * size)) & (row // size == col // size + 1)


def unit_inverse(block):
    row = lax.broadcasted_iota(jnp.int32, (SUB, SUB), 0)
    col = lax.broadcasted_iota(jnp.int32, (SUB, SUB), 1)
    inverse = jnp.where(row == col, 1.0, 0.0) - jnp.where(within(1), block, 0.0)
    size = 2
    while size < SUB // 2:
        below = jnp.where(within(size), block, 0.0).astype(BF16)
        inverse = inverse - mm_split(mm_exact(inverse, below), inverse)
        size *= 2
    return inverse


def kernel(
    a_hbm, b_hbm, rhs_hbm, panel_hbm, out_ref,
    a_v, b_v, bt, rhs_v, place, ut, yrecv, w, zrecv, g, lf, dall, mh, ml,
    load_b, load_a, load_s, y_s, y_r, z_s, z_r, gz_s, gz_r, gy_s, gy_r, px_s, px_r, pc_s, pc_r,
):
    row, col = lax.axis_index("row"), lax.axis_index("col")
    y, z = row // NZ, row % NZ
    x, core = col // 2, col % 2
    other = x * 2 + (1 - core)
    right = lax.rem(y + 1, NY) * NZ + z
    left = lax.rem(y + NY - 1, NY) * NZ + z
    depth, width = b_hbm.shape
    group = width // NY
    half = group // 2
    own = width // (NY * NZ)
    slab = panel_hbm.shape[1]

    def remote(src, dst, send, recv, r, c):
        return pltpu.make_async_remote_copy(
            src_ref=src, dst_ref=dst, send_sem=send, recv_sem=recv,
            device_id=(r, c), device_id_type=MESH,
        )

    def z_peer(d):
        return y * NZ + lax.rem(z + d, NZ)

    def y_peer(d):
        return lax.rem(y + d, NY) * NZ + z

    def z_rows(start, d):
        return pl.ds(pl.multiple_of(start + lax.rem(z + d, NZ) * own, own), own)

    def all_sent(sem, ref):
        remote(ref, ref, sem, sem, row, col).wait_send()

    def all_here(sem, ref):
        remote(ref, ref, sem, sem, row, col).wait_recv()

    def x_peer(d):
        return lax.rem(x + d, NX) * 2 + core

    barrier = pltpu.get_barrier_semaphore()

    def greet(r, c):
        pl.semaphore_signal(barrier, inc=1, device_id=(r, c), device_id_type=MESH)

    for d in Z_ORDER:
        greet(z_peer(d), col)
    for d in (2, 1, 3):
        greet(row, x_peer(d))
    for d in range(1, NY):
        greet(y_peer(d), col)
    greet(row, other)

    chunk = depth // CHUNKS
    load_panel = pltpu.make_async_copy(panel_hbm, lf.at[:, col], load_s.at[0])
    load_rhs = pltpu.make_async_copy(rhs_hbm, rhs_v, load_s.at[1])
    loads_b = [
        pltpu.make_async_copy(
            b_hbm.at[chunk * k : chunk * (k + 1), :], b_v.at[chunk * k : chunk * (k + 1), :], load_b.at[k]
        )
        for k in range(CHUNKS)
    ]

    def load(n):
        return pltpu.make_async_copy(a_hbm.at[:, PIECE * n : PIECE * (n + 1)], a_v.at[n], load_a.at[n])

    load_panel.start()
    for copy in loads_b:
        copy.start()
    load(3).start()
    load_rhs.start()

    load_panel.wait()
    at = pl.multiple_of(x * SUB, SUB)
    tiles = [lf[m, col, :, pl.ds(at, SUB)].astype(F32) for m in (0, 1)]
    turned = [pltpu.roll(tile, slab, 1) for tile in tiles]
    even = core == 0
    block = jnp.concatenate([jnp.where(even, tiles[0], turned[0]), jnp.where(even, turned[1], tiles[1])], axis=0)
    inverse = unit_inverse(block)
    dall[col] = inverse[:slab] + inverse[slab:]

    for k in range(CHUNKS):
        loads_b[k].wait()
        bt[:, chunk * k : chunk * (k + 1)] = b_v[chunk * k : chunk * (k + 1), :].T

    load(2).start()

    pl.semaphore_wait(barrier, (NY - 1) + (NZ - 1) + (NX - 1) + 1)

    def part(p, c):
        return dall.at[c] if p == 0 else lf.at[(1, 0, 2)[p - 1], c]

    def along_x(p, d):
        return remote(part(p, col), part(p, col), px_s.at[p], px_r.at[p, d - 1], row, x_peer(d))

    def across(p, d):
        shard = part(p, lax.rem(x + NX - d, NX) * 2 + core)
        return remote(shard, shard, pc_s.at[p], pc_r.at[p], row, other)

    def send_panel(p):
        for d in (2, 1, 3):
            along_x(p, d).start()
        across(p, 0).start()

    send_panel(0)
    send_panel(1)

    place[...] = jnp.zeros_like(place)
    load_rhs.wait()
    place[pl.ds(pl.multiple_of(z * (PIECE // NZ), 8), PIECE // NZ), :] = rhs_v[...]

    def y_group(target):
        return pl.multiple_of(target // NZ * group, group)

    right_rows, left_rows = y_group(right), y_group(left)
    far_rows = pl.multiple_of(lax.rem(y + 2, NY) * group, group)
    own_rows = pl.multiple_of(y * group, group)

    def y_copy(n, slot):
        start = ((right_rows, 1), (far_rows, 0), (right_rows, 0), (left_rows, 0), (far_rows, 1), (left_rows, 1))[slot]
        src = ut.at[n, pl.ds(start[0] + start[1] * half, half), :]
        target = right if slot < 3 else left
        return remote(src, yrecv.at[n, Y_SLOT[slot]], y_s, y_r.at[n, Y_SEM[slot]], target, col)

    def y_start(n, slots):
        for slot in slots:
            y_copy(n, slot).start()

    def update(n):
        load(n).wait()
        if n >= 2:
            load(n - 2).start()
        ut[n] = mm(bt[...], a_v[n])

        @pl.when(n == y)
        def _():
            ut[n] = ut[n] - place[...].T

    def relay(n):
        all_here(y_r.at[n, 0], yrecv.at[n, 0])
        ut[n, pl.ds(right_rows, half), :] += yrecv[n, 0]
        y_copy(n, 2).start()
        all_here(y_r.at[n, 1], yrecv.at[n, 1])
        ut[n, pl.ds(left_rows + half, half), :] += yrecv[n, 1]
        y_copy(n, 5).start()

    def z_copy(n, d):
        return remote(w.at[n, z_rows(0, d), :], zrecv.at[n, d - 1], z_s, z_r.at[n], z_peer(d), col)

    def y_sum(n):
        all_here(y_r.at[n, 2], yrecv.at[n, 2:6])
        w[n, :half, :] = ut[n, pl.ds(own_rows, half), :] + (yrecv[n, 3] + yrecv[n, 4])
        w[n, half:, :] = ut[n, pl.ds(own_rows + half, half), :] + (yrecv[n, 2] + yrecv[n, 5])
        for d in Z_ORDER:
            z_copy(n, d).start()

    def forward(p):
        for d in range(1, NX):
            along_x(p, d).wait_recv()
            across(p, d).start()

    def arrived(p):
        all_here(pc_r.at[p], dall.at[0:NX] if p == 0 else lf.at[0, 0:NX])

    update(3)
    y_start(3, (1, 4))
    update(2)
    y_start(2, (1, 4))
    y_start(3, (0, 3))
    update(1)
    y_start(1, (1, 4))
    relay(3)
    y_start(2, (0, 3))
    update(0)
    y_start(0, (1, 4))
    relay(2)
    y_start(1, (0, 3))
    send_panel(2)
    relay(1)
    y_start(0, (0, 3))
    forward(0)
    forward(1)
    y_sum(3)
    relay(0)
    send_panel(3)
    y_sum(2)
    y_sum(1)

    def whole_inverse(m):
        lane = lax.broadcasted_iota(jnp.int32, (slab, SUB), 1)

        def small(i):
            first, second = dall[2 * i], dall[2 * i + 1]
            if m == 0:
                second = pltpu.roll(second, slab, 1)
            else:
                first = pltpu.roll(first, slab, 1)
            first = jnp.where(lane < slab, first, 0.0)
            second = jnp.where(lane < slab, 0.0, second)
            value = jnp.concatenate([first, second], axis=0)
            diagonal = lower(i, i)
            below = jnp.where(within(slab), diagonal, jnp.zeros_like(diagonal))
            return value - mm_split(mm_exact(value, below), value)

        def lower(i, j):
            return lf[m, 2 * i : 2 * i + 2, :, SUB * j : SUB * (j + 1)].reshape(SUB, SUB)

        def pair(i):
            first, second = small(i), small(i + 1)
            below = -mm_split(mm_exact(second, lower(i + 1, i)), first)
            top = jnp.concatenate([first, jnp.zeros_like(first)], axis=1)
            return jnp.concatenate([top, jnp.concatenate([below, second], axis=1)], axis=0)

        first, second = pair(0), pair(2)
        off = lf[m, 4:, :, : 2 * SUB].reshape(2 * SUB, 2 * SUB)
        below = -mm_split(mm_exact(second, off), first)
        for rows, columns, value in (
            (slice(0, 2 * SUB), slice(0, 2 * SUB), first),
            (slice(0, 2 * SUB), slice(2 * SUB, BLOCK), jnp.zeros_like(first)),
            (slice(2 * SUB, BLOCK), slice(0, 2 * SUB), below),
            (slice(2 * SUB, BLOCK), slice(2 * SUB, BLOCK), second),
        ):
            high, low = split(value)
            mh[m, rows, columns] = high
            ml[m, rows, columns] = low

    def reduced(h):
        pieces = []
        for n in (2 * h, 2 * h + 1):
            all_here(z_r.at[n], zrecv.at[n])
            total = w[n, z_rows(0, 0), :]
            for d in range(1, NZ):
                total = total + zrecv[n, d - 1]
            pieces.append(-total)
        return jnp.concatenate(pieces, axis=1)

    def solve(h, value):
        return stacked(value, mh[h]) + mm(value.astype(BF16), ml[h])

    def gz_copy(h, d):
        rows = g.at[h, z_rows(own_rows, 0), :]
        return remote(rows, rows, gz_s, gz_r.at[h, 0 if d in NEAR else 1], z_peer(d), col)

    def spread(h, distances):
        for d in distances:
            rows = g.at[h, z_rows(own_rows, d), :]
            for side in (2, 1, 3):
                remote(rows, rows, gy_s, gy_r.at[h], y_peer(side), col).start()

    def publish(h, value):
        g[h, z_rows(own_rows, 0), :] = value
        for d in Z_ORDER:
            gz_copy(h, d).start()
        spread(h, (0,))

    def spread_near(h):
        all_here(gz_r.at[h, 0], g.at[h, 0 : 4 * own, :])
        spread(h, NEAR)

    def spread_far(h):
        all_here(gz_r.at[h, 1], g.at[h, 0 : 3 * own, :])
        spread(h, FAR)

    def finish(h):
        all_here(gy_r.at[h], g.at[h, 0 : 3 * group, :])
        out_ref[h * BLOCK : (h + 1) * BLOCK, :] = g[h].T

    arrived(0)
    arrived(1)
    whole_inverse(1)
    y_sum(0)
    forward(2)
    second = solve(1, reduced(1))
    publish(1, second)
    forward(3)
    arrived(2)
    whole_inverse(0)
    arrived(3)
    coupled = stacked(second, lf[2].reshape(BLOCK, BLOCK))
    first = solve(0, reduced(0) - coupled)
    publish(0, first)
    spread_near(1)
    spread_far(1)
    spread_near(0)
    spread_far(0)
    all_sent(y_s, yrecv)
    all_sent(z_s, zrecv)
    for p in range(PARTS):
        across_size = dall.at[0:NX] if p == 0 else lf.at[0, 0:NX]
        along_size = dall.at[0 : NX - 1] if p == 0 else lf.at[0, 0 : NX - 1]
        all_sent(px_s.at[p], along_size)
        all_sent(pc_s.at[p], across_size)
    finish(1)
    all_sent(gz_s, g.at[:, 0 : 7 * own, :])
    finish(0)
    all_sent(gy_s, g.at[:, 0 : 3 * group, :])


def shards(tail_factor, tail_solution, panel_rhs, panel_factor):
    depth, window = tail_factor.shape
    width = tail_solution.shape[1]
    group, own = width // NY, width // (NY * NZ)
    slab = panel_factor.shape[1]
    dma = pltpu.SemaphoreType.DMA
    scratch = [
        pltpu.VMEM((PIECES, depth, PIECE), BF16),
        pltpu.VMEM((depth, width), BF16),
        pltpu.VMEM((width, depth), BF16),
        pltpu.VMEM(panel_rhs.shape, F32),
        pltpu.VMEM((PIECE, width), F32),
        pltpu.VMEM((PIECES, width, PIECE), F32),
        pltpu.VMEM((PIECES, 6, group // 2, PIECE), F32),
        pltpu.VMEM((PIECES, group, PIECE), F32),
        pltpu.VMEM((PIECES, NZ - 1, own, PIECE), F32),
        pltpu.VMEM((2, width, BLOCK), F32),
        pltpu.VMEM((3, 2 * NX, slab, BLOCK), BF16),
        pltpu.VMEM((2 * NX, slab, SUB), F32),
        pltpu.VMEM((2, BLOCK, BLOCK), BF16),
        pltpu.VMEM((2, BLOCK, BLOCK), BF16),
        dma((CHUNKS,)), dma((PIECES,)), dma((2,)),
        dma, dma((PIECES, 3)),
        dma, dma((PIECES,)),
        dma, dma((2, 2)),
        dma, dma((2,)),
        dma((PARTS,)), dma((PARTS, NX - 1)),
        dma((PARTS,)), dma((PARTS,)),
    ]
    return pl.pallas_call(
        kernel,
        out_shape=jax.ShapeDtypeStruct((window, width), F32),
        in_specs=[pl.BlockSpec(memory_space=pltpu.HBM)] * 4,
        out_specs=pl.BlockSpec(memory_space=pltpu.VMEM),
        scratch_shapes=scratch,
        compiler_params=pltpu.CompilerParams(
            collective_id=0, has_side_effects=True, vmem_limit_bytes=60 * 1024 * 1024
        ),
    )(tail_factor, tail_solution, panel_rhs, panel_factor)


def solution(mesh):
    return jax.shard_map(
        shards,
        mesh=mesh,
        in_specs=(P("row", None), P("row", "col"), P("row", "col"), P(None, "col", None)),
        out_specs=P(None, "col"),
        check_vma=False,
    )
```

```python
import jax
import jax.numpy as jnp
from jax import lax
from jax.experimental import pallas as pl
from jax.experimental.pallas import tpu as pltpu
from jax.sharding import PartitionSpec as P

MESH = pl.DeviceIdType.MESH
F32 = jnp.float32
BF16 = jnp.bfloat16

NY, NZ, NX = 4, 8, 4
BLOCK = 512
WINDOW = 2 * BLOCK
PIECE = 256
PIECES = WINDOW // PIECE
SUB = 128
CHUNKS = 4
NEAR, FAR = (1, 7, 2, 6), (3, 5, 4)
Z_ORDER = (4, 3, 5, 2, 6, 1, 7)
WHOLE, FRONT, BACK = slice(0, BLOCK), slice(0, BLOCK // 2), slice(BLOCK // 2, BLOCK)
Y_SLOT = (2, 0, 3, 4, 1, 5)
Y_SEM = (2, 0, 2, 2, 1, 2)
PARTS = 4


def split(x):
    high = x.astype(BF16)
    return high, (x - high.astype(F32)).astype(BF16)


def mm(a, b):
    return jnp.dot(a, b, preferred_element_type=F32)


def mm_exact(a, b):
    high, low = split(a)
    return mm(high, b) + mm(low, b)


def mm_split(a, b):
    a_high, a_low = split(a)
    b_high, b_low = split(b)
    return mm(a_high, b_high) + (mm(a_low, b_high) + mm(a_high, b_low))


def stacked(a, b):
    rows = a.shape[0]
    both = mm(jnp.concatenate(split(a), axis=0), b)
    return both[:rows] + both[rows:]


def within(size):
    row = lax.broadcasted_iota(jnp.int32, (SUB, SUB), 0)
    col = lax.broadcasted_iota(jnp.int32, (SUB, SUB), 1)
    return (row // (2 * size) == col // (2 * size)) & (row // size == col // size + 1)


def unit_inverse(block):
    row = lax.broadcasted_iota(jnp.int32, (SUB, SUB), 0)
    col = lax.broadcasted_iota(jnp.int32, (SUB, SUB), 1)
    inverse = jnp.where(row == col, 1.0, 0.0) - jnp.where(within(1), block, 0.0)
    size = 2
    while size < SUB // 2:
        below = jnp.where(within(size), block, 0.0).astype(BF16)
        inverse = inverse - mm_split(mm_exact(inverse, below), inverse)
        size *= 2
    return inverse


def kernel(
    a_hbm, b_hbm, rhs_hbm, panel_hbm, out_ref,
    a_v, b_v, bt, rhs_v, place, ut, yrecv, w, zrecv, g, lf, dall, mh, ml,
    load_b, load_a, load_s, y_s, y_r, z_s, z_r, gz_s, gz_r, gy_s, gy_r, px_s, px_r, pc_s, pc_r,
):
    row, col = lax.axis_index("row"), lax.axis_index("col")
    y, z = row // NZ, row % NZ
    x, core = col // 2, col % 2
    other = x * 2 + (1 - core)
    right = lax.rem(y + 1, NY) * NZ + z
    left = lax.rem(y + NY - 1, NY) * NZ + z
    depth, width = b_hbm.shape
    group = width // NY
    half = group // 2
    own = width // (NY * NZ)
    slab = panel_hbm.shape[1]

    def remote(src, dst, send, recv, r, c):
        return pltpu.make_async_remote_copy(
            src_ref=src, dst_ref=dst, send_sem=send, recv_sem=recv,
            device_id=(r, c), device_id_type=MESH,
        )

    def z_peer(d):
        return y * NZ + lax.rem(z + d, NZ)

    def y_peer(d):
        return lax.rem(y + d, NY) * NZ + z

    def z_rows(start, d):
        return pl.ds(pl.multiple_of(start + lax.rem(z + d, NZ) * own, own), own)

    def all_sent(sem, ref):
        remote(ref, ref, sem, sem, row, col).wait_send()

    def all_here(sem, ref):
        remote(ref, ref, sem, sem, row, col).wait_recv()

    def x_peer(d):
        return lax.rem(x + d, NX) * 2 + core

    barrier = pltpu.get_barrier_semaphore()

    def greet(r, c):
        pl.semaphore_signal(barrier, inc=1, device_id=(r, c), device_id_type=MESH)

    for d in Z_ORDER:
        greet(z_peer(d), col)
    for d in (2, 1, 3):
        greet(row, x_peer(d))
    for d in range(1, NY):
        greet(y_peer(d), col)
    greet(row, other)

    chunk = depth // CHUNKS
    load_panel = pltpu.make_async_copy(panel_hbm, lf.at[:, col], load_s.at[0])
    load_rhs = pltpu.make_async_copy(rhs_hbm, rhs_v, load_s.at[1])
    loads_b = [
        pltpu.make_async_copy(
            b_hbm.at[chunk * k : chunk * (k + 1), :], b_v.at[chunk * k : chunk * (k + 1), :], load_b.at[k]
        )
        for k in range(CHUNKS)
    ]

    def load(n):
        return pltpu.make_async_copy(a_hbm.at[:, PIECE * n : PIECE * (n + 1)], a_v.at[n], load_a.at[n])

    load_panel.start()
    for copy in loads_b:
        copy.start()
    load(3).start()
    load_rhs.start()

    load_panel.wait()
    at = pl.multiple_of(x * SUB, SUB)
    tiles = [lf[m, col, :, pl.ds(at, SUB)].astype(F32) for m in (0, 1)]
    turned = [pltpu.roll(tile, slab, 1) for tile in tiles]
    even = core == 0
    block = jnp.concatenate([jnp.where(even, tiles[0], turned[0]), jnp.where(even, turned[1], tiles[1])], axis=0)
    inverse = unit_inverse(block)
    dall[col] = inverse[:slab] + inverse[slab:]

    for k in range(CHUNKS):
        loads_b[k].wait()
        bt[:, chunk * k : chunk * (k + 1)] = b_v[chunk * k : chunk * (k + 1), :].T

    load(2).start()

    pl.semaphore_wait(barrier, (NY - 1) + (NZ - 1) + (NX - 1) + 1)

    def part(p, c):
        return dall.at[c] if p == 0 else lf.at[(1, 0, 2)[p - 1], c]

    def along_x(p, d):
        return remote(part(p, col), part(p, col), px_s.at[p], px_r.at[p, d - 1], row, x_peer(d))

    def across(p, d):
        shard = part(p, lax.rem(x + NX - d, NX) * 2 + core)
        return remote(shard, shard, pc_s.at[p], pc_r.at[p], row, other)

    def send_panel(p):
        for d in (2, 1, 3):
            along_x(p, d).start()
        across(p, 0).start()

    send_panel(0)
    send_panel(1)

    place[...] = jnp.zeros_like(place)
    load_rhs.wait()
    place[pl.ds(pl.multiple_of(z * (PIECE // NZ), 8), PIECE // NZ), :] = rhs_v[...]

    def y_group(target):
        return pl.multiple_of(target // NZ * group, group)

    right_rows, left_rows = y_group(right), y_group(left)
    far_rows = pl.multiple_of(lax.rem(y + 2, NY) * group, group)
    own_rows = pl.multiple_of(y * group, group)

    def y_copy(n, slot):
        start = ((right_rows, 1), (far_rows, 0), (right_rows, 0), (left_rows, 0), (far_rows, 1), (left_rows, 1))[slot]
        src = ut.at[n, pl.ds(start[0] + start[1] * half, half), :]
        target = right if slot < 3 else left
        return remote(src, yrecv.at[n, Y_SLOT[slot]], y_s, y_r.at[n, Y_SEM[slot]], target, col)

    def y_start(n, slots):
        for slot in slots:
            y_copy(n, slot).start()

    def update(n):
        load(n).wait()
        if n >= 2:
            load(n - 2).start()
        ut[n] = mm(bt[...], a_v[n])

        @pl.when(n == y)
        def _():
            ut[n] = ut[n] - place[...].T

    def relay(n):
        all_here(y_r.at[n, 0], yrecv.at[n, 0])
        ut[n, pl.ds(right_rows, half), :] += yrecv[n, 0]
        y_copy(n, 2).start()
        all_here(y_r.at[n, 1], yrecv.at[n, 1])
        ut[n, pl.ds(left_rows + half, half), :] += yrecv[n, 1]
        y_copy(n, 5).start()

    def z_copy(n, d):
        return remote(w.at[n, z_rows(0, d), :], zrecv.at[n, d - 1], z_s, z_r.at[n], z_peer(d), col)

    def y_sum(n):
        all_here(y_r.at[n, 2], yrecv.at[n, 2:6])
        w[n, :half, :] = ut[n, pl.ds(own_rows, half), :] + (yrecv[n, 3] + yrecv[n, 4])
        w[n, half:, :] = ut[n, pl.ds(own_rows + half, half), :] + (yrecv[n, 2] + yrecv[n, 5])
        for d in Z_ORDER:
            z_copy(n, d).start()

    def forward(p):
        for d in range(1, NX):
            along_x(p, d).wait_recv()
            across(p, d).start()

    def arrived(p):
        all_here(pc_r.at[p], dall.at[0:NX] if p == 0 else lf.at[0, 0:NX])

    update(3)
    y_start(3, (1, 4))
    update(2)
    y_start(2, (1, 4))
    y_start(3, (0, 3))
    update(1)
    y_start(1, (1, 4))
    relay(3)
    y_start(2, (0, 3))
    update(0)
    y_start(0, (1, 4))
    relay(2)
    y_start(1, (0, 3))
    send_panel(2)
    relay(1)
    y_start(0, (0, 3))
    forward(0)
    forward(1)
    y_sum(3)
    relay(0)
    send_panel(3)
    y_sum(2)
    y_sum(1)
    forward(2)

    def whole_inverse(m):
        lane = lax.broadcasted_iota(jnp.int32, (slab, SUB), 1)

        def small(i):
            first, second = dall[2 * i], dall[2 * i + 1]
            if m == 0:
                second = pltpu.roll(second, slab, 1)
            else:
                first = pltpu.roll(first, slab, 1)
            first = jnp.where(lane < slab, first, 0.0)
            second = jnp.where(lane < slab, 0.0, second)
            value = jnp.concatenate([first, second], axis=0)
            diagonal = lower(i, i)
            below = jnp.where(within(slab), diagonal, jnp.zeros_like(diagonal))
            return value - mm_split(mm_exact(value, below), value)

        def lower(i, j):
            return lf[m, 2 * i : 2 * i + 2, :, SUB * j : SUB * (j + 1)].reshape(SUB, SUB)

        def pair(i):
            first, second = small(i), small(i + 1)
            below = -mm_split(mm_exact(second, lower(i + 1, i)), first)
            top = jnp.concatenate([first, jnp.zeros_like(first)], axis=1)
            return jnp.concatenate([top, jnp.concatenate([below, second], axis=1)], axis=0)

        first, second = pair(0), pair(2)
        off = lf[m, 4:, :, : 2 * SUB].reshape(2 * SUB, 2 * SUB)
        below = -mm_split(mm_exact(second, off), first)
        for rows, columns, value in (
            (slice(0, 2 * SUB), slice(0, 2 * SUB), first),
            (slice(0, 2 * SUB), slice(2 * SUB, BLOCK), jnp.zeros_like(first)),
            (slice(2 * SUB, BLOCK), slice(0, 2 * SUB), below),
            (slice(2 * SUB, BLOCK), slice(2 * SUB, BLOCK), second),
        ):
            high, low = split(value)
            mh[m, rows, columns] = high
            ml[m, rows, columns] = low

    def reduced(h):
        pieces = []
        for n in (2 * h, 2 * h + 1):
            all_here(z_r.at[n], zrecv.at[n])
            total = w[n, z_rows(0, 0), :]
            for d in range(1, NZ):
                total = total + zrecv[n, d - 1]
            pieces.append(-total)
        return jnp.concatenate(pieces, axis=1)

    def solve(h, value):
        return stacked(value, mh[h]) + mm(value.astype(BF16), ml[h])

    def gz_copy(h, d):
        rows = g.at[h, z_rows(own_rows, 0), :]
        return remote(rows, rows, gz_s, gz_r.at[h, 0 if d in NEAR else 1], z_peer(d), col)

    def gy_copy(h, d, start, columns, sem, side):
        rows = g.at[h, z_rows(start, d), columns]
        return remote(rows, rows, gy_s, gy_r.at[h, sem], y_peer(side), col)

    def spread(h, distances, wave):
        for d in distances:
            gy_copy(h, d, own_rows, WHOLE, wave, 1).start()
            gy_copy(h, d, own_rows, WHOLE, 3 + wave, 3).start()

    def pass_on(h, distances, wave):
        size = g.at[h, 0 : len(distances) * own, :]
        all_here(gy_r.at[h, wave], size)
        for d in distances:
            gy_copy(h, d, left_rows, FRONT, 6, 1).start()
        all_here(gy_r.at[h, 3 + wave], size)
        for d in distances:
            gy_copy(h, d, right_rows, BACK, 6, 3).start()

    def publish(h, value):
        g[h, z_rows(own_rows, 0), :] = value
        for d in Z_ORDER:
            gz_copy(h, d).start()
        spread(h, (0,), 0)

    def spread_near(h):
        all_here(gz_r.at[h, 0], g.at[h, 0 : 4 * own, :])
        spread(h, NEAR, 1)

    def spread_far(h):
        all_here(gz_r.at[h, 1], g.at[h, 0 : 3 * own, :])
        if h == 0:
            for d in FAR:
                gy_copy(h, d, own_rows, WHOLE, 6, 2).start()
        spread(h, FAR, 2)

    def finish(h):
        if h == 0:
            all_here(gy_r.at[h, 2], g.at[h, 0 : 3 * own, :])
            all_here(gy_r.at[h, 5], g.at[h, 0 : 3 * own, :])
        all_here(gy_r.at[h, 6], g.at[h, 0:group, :])
        out_ref[h * BLOCK : (h + 1) * BLOCK, :] = g[h].T

    arrived(0)
    arrived(1)
    whole_inverse(1)
    y_sum(0)
    forward(3)
    arrived(2)
    whole_inverse(0)
    second = solve(1, reduced(1))
    publish(1, second)
    arrived(3)
    coupled = stacked(second, lf[2].reshape(BLOCK, BLOCK))
    first = solve(0, reduced(0) - coupled)
    publish(0, first)
    pass_on(1, (0,), 0)
    spread_near(1)
    spread_far(1)
    spread_near(0)
    pass_on(1, NEAR, 1)
    pass_on(0, (0,), 0)
    spread_far(0)
    pass_on(1, FAR, 2)
    all_sent(y_s, yrecv)
    all_sent(z_s, zrecv)
    for p in range(PARTS):
        across_size = dall.at[0:NX] if p == 0 else lf.at[0, 0:NX]
        along_size = dall.at[0 : NX - 1] if p == 0 else lf.at[0, 0 : NX - 1]
        all_sent(px_s.at[p], along_size)
        all_sent(pc_s.at[p], across_size)
    pass_on(0, NEAR, 1)
    finish(1)
    all_sent(gz_s, g.at[:, 0 : 7 * own, :])
    finish(0)
    all_sent(gy_s, g.at[:, 0 : 3 * group, :])


def shards(tail_factor, tail_solution, panel_rhs, panel_factor):
    depth, window = tail_factor.shape
    width = tail_solution.shape[1]
    group, own = width // NY, width // (NY * NZ)
    slab = panel_factor.shape[1]
    dma = pltpu.SemaphoreType.DMA
    scratch = [
        pltpu.VMEM((PIECES, depth, PIECE), BF16),
        pltpu.VMEM((depth, width), BF16),
        pltpu.VMEM((width, depth), BF16),
        pltpu.VMEM(panel_rhs.shape, F32),
        pltpu.VMEM((PIECE, width), F32),
        pltpu.VMEM((PIECES, width, PIECE), F32),
        pltpu.VMEM((PIECES, 6, group // 2, PIECE), F32),
        pltpu.VMEM((PIECES, group, PIECE), F32),
        pltpu.VMEM((PIECES, NZ - 1, own, PIECE), F32),
        pltpu.VMEM((2, width, BLOCK), F32),
        pltpu.VMEM((3, 2 * NX, slab, BLOCK), BF16),
        pltpu.VMEM((2 * NX, slab, SUB), F32),
        pltpu.VMEM((2, BLOCK, BLOCK), BF16),
        pltpu.VMEM((2, BLOCK, BLOCK), BF16),
        dma((CHUNKS,)), dma((PIECES,)), dma((2,)),
        dma, dma((PIECES, 3)),
        dma, dma((PIECES,)),
        dma, dma((2, 2)),
        dma, dma((2, 7)),
        dma((PARTS,)), dma((PARTS, NX - 1)),
        dma((PARTS,)), dma((PARTS,)),
    ]
    return pl.pallas_call(
        kernel,
        out_shape=jax.ShapeDtypeStruct((window, width), F32),
        in_specs=[pl.BlockSpec(memory_space=pltpu.HBM)] * 4,
        out_specs=pl.BlockSpec(memory_space=pltpu.VMEM),
        scratch_shapes=scratch,
        compiler_params=pltpu.CompilerParams(
            collective_id=0, has_side_effects=True, vmem_limit_bytes=52 * 1024 * 1024
        ),
    )(tail_factor, tail_solution, panel_rhs, panel_factor)


def solution(mesh):
    return jax.shard_map(
        shards,
        mesh=mesh,
        in_specs=(P("row", None), P("row", "col"), P("row", "col"), P(None, "col", None)),
        out_specs=P(None, "col"),
        check_vma=False,
    )
```

```python
import jax
import jax.numpy as jnp
from jax import lax
from jax.experimental import pallas as pl
from jax.experimental.pallas import tpu as pltpu
from jax.sharding import PartitionSpec as P

MESH = pl.DeviceIdType.MESH
F32 = jnp.float32
BF16 = jnp.bfloat16

NY, NZ, NX = 4, 8, 4
BLOCK = 512
WINDOW = 2 * BLOCK
PIECE = 256
PIECES = WINDOW // PIECE
SUB = 128
CHUNKS = 4
NEAR, FAR = (1, 7, 2, 6), (3, 5, 4)
Z_ORDER = (4, 3, 5, 2, 6, 1, 7)
WHOLE, FRONT, BACK = slice(0, BLOCK), slice(0, BLOCK // 2), slice(BLOCK // 2, BLOCK)
Y_SLOT = (2, 0, 3, 4, 1, 5)
Y_SEM = (2, 0, 2, 2, 1, 2)
PARTS = 4


def split(x):
    high = x.astype(BF16)
    return high, (x - high.astype(F32)).astype(BF16)


def mm(a, b):
    return jnp.dot(a, b, preferred_element_type=F32)


def mm_exact(a, b):
    high, low = split(a)
    return mm(high, b) + mm(low, b)


def mm_split(a, b):
    a_high, a_low = split(a)
    b_high, b_low = split(b)
    return mm(a_high, b_high) + (mm(a_low, b_high) + mm(a_high, b_low))


def stacked(a, b):
    rows = a.shape[0]
    both = mm(jnp.concatenate(split(a), axis=0), b)
    return both[:rows] + both[rows:]


def within(size):
    row = lax.broadcasted_iota(jnp.int32, (SUB, SUB), 0)
    col = lax.broadcasted_iota(jnp.int32, (SUB, SUB), 1)
    return (row // (2 * size) == col // (2 * size)) & (row // size == col // size + 1)


def unit_inverse(block):
    row = lax.broadcasted_iota(jnp.int32, (SUB, SUB), 0)
    col = lax.broadcasted_iota(jnp.int32, (SUB, SUB), 1)
    inverse = jnp.where(row == col, 1.0, 0.0) - jnp.where(within(1), block, 0.0)
    size = 2
    while size < SUB // 2:
        below = jnp.where(within(size), block, 0.0).astype(BF16)
        inverse = inverse - mm_split(mm_exact(inverse, below), inverse)
        size *= 2
    return inverse


def kernel(
    a_hbm, b_hbm, rhs_hbm, panel_hbm, out_ref,
    a_v, b_v, bt, rhs_v, place, ut, yrecv, w, zrecv, g, lf, dall, mh, ml,
    load_b, load_a, load_s, y_s, y_r, z_s, z_r, gz_s, gz_r, gy_s, gy_r, px_s, px_r, pc_s, pc_r,
):
    row, col = lax.axis_index("row"), lax.axis_index("col")
    y, z = row // NZ, row % NZ
    x, core = col // 2, col % 2
    other = x * 2 + (1 - core)
    right = lax.rem(y + 1, NY) * NZ + z
    left = lax.rem(y + NY - 1, NY) * NZ + z
    depth, width = b_hbm.shape
    group = width // NY
    half = group // 2
    own = width // (NY * NZ)
    slab = panel_hbm.shape[1]

    def remote(src, dst, send, recv, r, c):
        return pltpu.make_async_remote_copy(
            src_ref=src, dst_ref=dst, send_sem=send, recv_sem=recv,
            device_id=(r, c), device_id_type=MESH,
        )

    def z_peer(d):
        return y * NZ + lax.rem(z + d, NZ)

    def y_peer(d):
        return lax.rem(y + d, NY) * NZ + z

    def z_rows(start, d):
        return pl.ds(pl.multiple_of(start + lax.rem(z + d, NZ) * own, own), own)

    def all_sent(sem, ref):
        remote(ref, ref, sem, sem, row, col).wait_send()

    def all_here(sem, ref):
        remote(ref, ref, sem, sem, row, col).wait_recv()

    def x_peer(d):
        return lax.rem(x + d, NX) * 2 + core

    barrier = pltpu.get_barrier_semaphore()

    def greet(r, c):
        pl.semaphore_signal(barrier, inc=1, device_id=(r, c), device_id_type=MESH)

    for d in Z_ORDER:
        greet(z_peer(d), col)
    for d in (2, 1, 3):
        greet(row, x_peer(d))
    for d in range(1, NY):
        greet(y_peer(d), col)
    greet(row, other)

    chunk = depth // CHUNKS
    load_panel = pltpu.make_async_copy(panel_hbm, lf.at[:, col], load_s.at[0])
    load_rhs = pltpu.make_async_copy(rhs_hbm, rhs_v, load_s.at[1])
    loads_b = [
        pltpu.make_async_copy(
            b_hbm.at[chunk * k : chunk * (k + 1), :], b_v.at[chunk * k : chunk * (k + 1), :], load_b.at[k]
        )
        for k in range(CHUNKS)
    ]

    def load(n):
        return pltpu.make_async_copy(a_hbm.at[:, PIECE * n : PIECE * (n + 1)], a_v.at[n], load_a.at[n])

    load_panel.start()
    for copy in loads_b:
        copy.start()
    load(3).start()
    load_rhs.start()

    load_panel.wait()
    at = pl.multiple_of(x * SUB, SUB)
    tiles = [lf[m, col, :, pl.ds(at, SUB)].astype(F32) for m in (0, 1)]
    turned = [pltpu.roll(tile, slab, 1) for tile in tiles]
    even = core == 0
    block = jnp.concatenate([jnp.where(even, tiles[0], turned[0]), jnp.where(even, turned[1], tiles[1])], axis=0)
    inverse = unit_inverse(block)
    dall[col] = inverse[:slab] + inverse[slab:]

    for k in range(CHUNKS):
        loads_b[k].wait()
        bt[:, chunk * k : chunk * (k + 1)] = b_v[chunk * k : chunk * (k + 1), :].T

    load(2).start()

    pl.semaphore_wait(barrier, (NY - 1) + (NZ - 1) + (NX - 1) + 1)

    def part(p, c):
        return dall.at[c] if p == 0 else lf.at[(1, 0, 2)[p - 1], c]

    def along_x(p, d):
        return remote(part(p, col), part(p, col), px_s.at[p], px_r.at[p, d - 1], row, x_peer(d))

    def across(p, d):
        shard = part(p, lax.rem(x + NX - d, NX) * 2 + core)
        return remote(shard, shard, pc_s.at[p], pc_r.at[p], row, other)

    def send_panel(p):
        for d in (2, 1, 3):
            along_x(p, d).start()
        across(p, 0).start()

    send_panel(0)
    send_panel(1)

    place[...] = jnp.zeros_like(place)
    load_rhs.wait()
    place[pl.ds(pl.multiple_of(z * (PIECE // NZ), 8), PIECE // NZ), :] = rhs_v[...]

    def y_group(target):
        return pl.multiple_of(target // NZ * group, group)

    right_rows, left_rows = y_group(right), y_group(left)
    far_rows = pl.multiple_of(lax.rem(y + 2, NY) * group, group)
    own_rows = pl.multiple_of(y * group, group)

    def y_copy(n, slot):
        start = ((right_rows, 1), (far_rows, 0), (right_rows, 0), (left_rows, 0), (far_rows, 1), (left_rows, 1))[slot]
        src = ut.at[n, pl.ds(start[0] + start[1] * half, half), :]
        target = right if slot < 3 else left
        return remote(src, yrecv.at[n, Y_SLOT[slot]], y_s, y_r.at[n, Y_SEM[slot]], target, col)

    def y_start(n, slots):
        for slot in slots:
            y_copy(n, slot).start()

    def update(n):
        load(n).wait()
        if n >= 2:
            load(n - 2).start()
        ut[n] = mm(bt[...], a_v[n])

        @pl.when(n == y)
        def _():
            ut[n] = ut[n] - place[...].T

    def relay(n):
        all_here(y_r.at[n, 0], yrecv.at[n, 0])
        ut[n, pl.ds(right_rows, half), :] += yrecv[n, 0]
        y_copy(n, 2).start()
        all_here(y_r.at[n, 1], yrecv.at[n, 1])
        ut[n, pl.ds(left_rows + half, half), :] += yrecv[n, 1]
        y_copy(n, 5).start()

    def z_copy(n, d):
        return remote(w.at[n, z_rows(0, d), :], zrecv.at[n, d - 1], z_s, z_r.at[n], z_peer(d), col)

    def y_sum(n):
        all_here(y_r.at[n, 2], yrecv.at[n, 2:6])
        w[n, :half, :] = ut[n, pl.ds(own_rows, half), :] + (yrecv[n, 3] + yrecv[n, 4])
        w[n, half:, :] = ut[n, pl.ds(own_rows + half, half), :] + (yrecv[n, 2] + yrecv[n, 5])
        for d in Z_ORDER:
            z_copy(n, d).start()

    def forward(p):
        for d in range(1, NX):
            along_x(p, d).wait_recv()
            across(p, d).start()

    def arrived(p):
        all_here(pc_r.at[p], dall.at[0:NX] if p == 0 else lf.at[0, 0:NX])

    update(3)
    y_start(3, (1, 4))
    update(2)
    y_start(2, (1, 4))
    y_start(3, (0, 3))
    update(1)
    y_start(1, (1, 4))
    relay(3)
    y_start(2, (0, 3))
    update(0)
    y_start(0, (1, 4))
    relay(2)
    y_start(1, (0, 3))
    send_panel(2)
    relay(1)
    y_start(0, (0, 3))
    forward(0)
    forward(1)
    y_sum(3)
    relay(0)
    send_panel(3)
    y_sum(2)
    y_sum(1)

    def whole_inverse(m):
        lane = lax.broadcasted_iota(jnp.int32, (slab, SUB), 1)

        def small(i):
            first, second = dall[2 * i], dall[2 * i + 1]
            if m == 0:
                second = pltpu.roll(second, slab, 1)
            else:
                first = pltpu.roll(first, slab, 1)
            first = jnp.where(lane < slab, first, 0.0)
            second = jnp.where(lane < slab, 0.0, second)
            value = jnp.concatenate([first, second], axis=0)
            diagonal = lower(i, i)
            below = jnp.where(within(slab), diagonal, jnp.zeros_like(diagonal))
            return value - mm_split(mm_exact(value, below), value)

        def lower(i, j):
            return lf[m, 2 * i : 2 * i + 2, :, SUB * j : SUB * (j + 1)].reshape(SUB, SUB)

        def pair(i):
            first, second = small(i), small(i + 1)
            below = -mm_split(mm_exact(second, lower(i + 1, i)), first)
            top = jnp.concatenate([first, jnp.zeros_like(first)], axis=1)
            return jnp.concatenate([top, jnp.concatenate([below, second], axis=1)], axis=0)

        first, second = pair(0), pair(2)
        off = lf[m, 4:, :, : 2 * SUB].reshape(2 * SUB, 2 * SUB)
        below = -mm_split(mm_exact(second, off), first)
        for rows, columns, value in (
            (slice(0, 2 * SUB), slice(0, 2 * SUB), first),
            (slice(0, 2 * SUB), slice(2 * SUB, BLOCK), jnp.zeros_like(first)),
            (slice(2 * SUB, BLOCK), slice(0, 2 * SUB), below),
            (slice(2 * SUB, BLOCK), slice(2 * SUB, BLOCK), second),
        ):
            high, low = split(value)
            mh[m, rows, columns] = high
            ml[m, rows, columns] = low

    def reduced(h):
        pieces = []
        for n in (2 * h, 2 * h + 1):
            all_here(z_r.at[n], zrecv.at[n])
            total = w[n, z_rows(0, 0), :]
            for d in range(1, NZ):
                total = total + zrecv[n, d - 1]
            pieces.append(-total)
        return jnp.concatenate(pieces, axis=1)

    def solve(h, value):
        return stacked(value, mh[h]) + mm(value.astype(BF16), ml[h])

    def gz_copy(h, d):
        rows = g.at[h, z_rows(own_rows, 0), :]
        return remote(rows, rows, gz_s, gz_r.at[h, 0 if d in NEAR else 1], z_peer(d), col)

    def gy_copy(h, d, start, columns, sem, side):
        rows = g.at[h, z_rows(start, d), columns]
        return remote(rows, rows, gy_s, gy_r.at[h, sem], y_peer(side), col)

    def spread(h, distances, wave):
        for d in distances:
            gy_copy(h, d, own_rows, WHOLE, wave, 1).start()
            gy_copy(h, d, own_rows, WHOLE, 3 + wave, 3).start()

    def pass_on(h, distances, wave):
        size = g.at[h, 0 : len(distances) * own, :]
        all_here(gy_r.at[h, wave], size)
        for d in distances:
            gy_copy(h, d, left_rows, FRONT, 6, 1).start()
        all_here(gy_r.at[h, 3 + wave], size)
        for d in distances:
            gy_copy(h, d, right_rows, BACK, 6, 3).start()

    def publish(h, value):
        g[h, z_rows(own_rows, 0), :] = value
        for d in Z_ORDER:
            gz_copy(h, d).start()
        spread(h, (0,), 0)

    def spread_near(h):
        all_here(gz_r.at[h, 0], g.at[h, 0 : 4 * own, :])
        spread(h, NEAR, 1)

    def spread_far(h):
        all_here(gz_r.at[h, 1], g.at[h, 0 : 3 * own, :])
        if h == 0:
            for d in FAR:
                gy_copy(h, d, own_rows, WHOLE, 6, 2).start()
        spread(h, FAR, 2)

    def finish(h):
        if h == 0:
            all_here(gy_r.at[h, 2], g.at[h, 0 : 3 * own, :])
            all_here(gy_r.at[h, 5], g.at[h, 0 : 3 * own, :])
        all_here(gy_r.at[h, 6], g.at[h, 0:group, :])
        out_ref[h * BLOCK : (h + 1) * BLOCK, :] = g[h].T

    arrived(0)
    arrived(1)
    whole_inverse(1)
    y_sum(0)
    forward(2)
    second = solve(1, reduced(1))
    publish(1, second)
    forward(3)
    arrived(2)
    whole_inverse(0)
    arrived(3)
    coupled = stacked(second, lf[2].reshape(BLOCK, BLOCK))
    first = solve(0, reduced(0) - coupled)
    publish(0, first)
    pass_on(1, (0,), 0)
    spread_near(1)
    spread_far(1)
    spread_near(0)
    pass_on(1, NEAR, 1)
    pass_on(0, (0,), 0)
    spread_far(0)
    pass_on(1, FAR, 2)
    all_sent(y_s, yrecv)
    all_sent(z_s, zrecv)
    for p in range(PARTS):
        across_size = dall.at[0:NX] if p == 0 else lf.at[0, 0:NX]
        along_size = dall.at[0 : NX - 1] if p == 0 else lf.at[0, 0 : NX - 1]
        all_sent(px_s.at[p], along_size)
        all_sent(pc_s.at[p], across_size)
    pass_on(0, NEAR, 1)
    finish(1)
    all_sent(gz_s, g.at[:, 0 : 7 * own, :])
    finish(0)
    all_sent(gy_s, g.at[:, 0 : 3 * group, :])


def shards(tail_factor, tail_solution, panel_rhs, panel_factor):
    depth, window = tail_factor.shape
    width = tail_solution.shape[1]
    group, own = width // NY, width // (NY * NZ)
    slab = panel_factor.shape[1]
    dma = pltpu.SemaphoreType.DMA
    scratch = [
        pltpu.VMEM((PIECES, depth, PIECE), BF16),
        pltpu.VMEM((depth, width), BF16),
        pltpu.VMEM((width, depth), BF16),
        pltpu.VMEM(panel_rhs.shape, F32),
        pltpu.VMEM((PIECE, width), F32),
        pltpu.VMEM((PIECES, width, PIECE), F32),
        pltpu.VMEM((PIECES, 6, group // 2, PIECE), F32),
        pltpu.VMEM((PIECES, group, PIECE), F32),
        pltpu.VMEM((PIECES, NZ - 1, own, PIECE), F32),
        pltpu.VMEM((2, width, BLOCK), F32),
        pltpu.VMEM((3, 2 * NX, slab, BLOCK), BF16),
        pltpu.VMEM((2 * NX, slab, SUB), F32),
        pltpu.VMEM((2, BLOCK, BLOCK), BF16),
        pltpu.VMEM((2, BLOCK, BLOCK), BF16),
        dma((CHUNKS,)), dma((PIECES,)), dma((2,)),
        dma, dma((PIECES, 3)),
        dma, dma((PIECES,)),
        dma, dma((2, 2)),
        dma, dma((2, 7)),
        dma((PARTS,)), dma((PARTS, NX - 1)),
        dma((PARTS,)), dma((PARTS,)),
    ]
    return pl.pallas_call(
        kernel,
        out_shape=jax.ShapeDtypeStruct((window, width), F32),
        in_specs=[pl.BlockSpec(memory_space=pltpu.HBM)] * 4,
        out_specs=pl.BlockSpec(memory_space=pltpu.VMEM),
        scratch_shapes=scratch,
        compiler_params=pltpu.CompilerParams(
            collective_id=0, has_side_effects=True, vmem_limit_bytes=52 * 1024 * 1024
        ),
    )(tail_factor, tail_solution, panel_rhs, panel_factor)


def solution(mesh):
    return jax.shard_map(
        shards,
        mesh=mesh,
        in_specs=(P("row", None), P("row", "col"), P("row", "col"), P(None, "col", None)),
        out_specs=P(None, "col"),
        check_vma=False,
    )
```

```python
import jax
import jax.numpy as jnp
from jax import lax
from jax.experimental import pallas as pl
from jax.experimental.pallas import tpu as pltpu
from jax.sharding import PartitionSpec as P

MESH = pl.DeviceIdType.MESH
F32 = jnp.float32
BF16 = jnp.bfloat16

NY, NZ, NX = 4, 8, 4
BLOCK = 512
WINDOW = 2 * BLOCK
PIECE = 256
PIECES = WINDOW // PIECE
SUB = 128
CHUNKS = 4
NEAR, FAR = (1, 7, 2, 6), (3, 5, 4)
Z_ORDER = (4, 3, 5, 2, 6, 1, 7)
WHOLE, FRONT, BACK = slice(0, BLOCK), slice(0, BLOCK // 2), slice(BLOCK // 2, BLOCK)
Y_SLOT = (2, 0, 3, 4, 1, 5)
Y_SEM = (2, 0, 2, 2, 1, 2)
PARTS = 4


def split(x):
    high = x.astype(BF16)
    return high, (x - high.astype(F32)).astype(BF16)


def mm(a, b):
    return jnp.dot(a, b, preferred_element_type=F32)


def mm_exact(a, b):
    high, low = split(a)
    return mm(high, b) + mm(low, b)


def mm_split(a, b):
    a_high, a_low = split(a)
    b_high, b_low = split(b)
    return mm(a_high, b_high) + (mm(a_low, b_high) + mm(a_high, b_low))


def stacked(a, b):
    rows = a.shape[0]
    both = mm(jnp.concatenate(split(a), axis=0), b)
    return both[:rows] + both[rows:]


def within(size):
    row = lax.broadcasted_iota(jnp.int32, (SUB, SUB), 0)
    col = lax.broadcasted_iota(jnp.int32, (SUB, SUB), 1)
    return (row // (2 * size) == col // (2 * size)) & (row // size == col // size + 1)


def unit_inverse(block):
    row = lax.broadcasted_iota(jnp.int32, (SUB, SUB), 0)
    col = lax.broadcasted_iota(jnp.int32, (SUB, SUB), 1)
    inverse = jnp.where(row == col, 1.0, 0.0) - jnp.where(within(1), block, 0.0)
    size = 2
    while size < SUB // 2:
        below = jnp.where(within(size), block, 0.0).astype(BF16)
        inverse = inverse - mm_split(mm_exact(inverse, below), inverse)
        size *= 2
    return inverse


def kernel(
    a_hbm, b_hbm, rhs_hbm, panel_hbm, out_ref,
    a_v, b_v, bt, rhs_v, place, ut, yrecv, w, zrecv, g, lf, dall, mh, ml,
    load_b, load_a, load_s, y_s, y_r, z_s, z_r, gz_s, gz_r, gy_s, gy_r, px_s, px_r, pc_s, pc_r,
):
    row, col = lax.axis_index("row"), lax.axis_index("col")
    y, z = row // NZ, row % NZ
    x, core = col // 2, col % 2
    other = x * 2 + (1 - core)
    right = lax.rem(y + 1, NY) * NZ + z
    left = lax.rem(y + NY - 1, NY) * NZ + z
    depth, width = b_hbm.shape
    group = width // NY
    half = group // 2
    own = width // (NY * NZ)
    slab = panel_hbm.shape[1]

    def remote(src, dst, send, recv, r, c):
        return pltpu.make_async_remote_copy(
            src_ref=src, dst_ref=dst, send_sem=send, recv_sem=recv,
            device_id=(r, c), device_id_type=MESH,
        )

    def z_peer(d):
        return y * NZ + lax.rem(z + d, NZ)

    def y_peer(d):
        return lax.rem(y + d, NY) * NZ + z

    def z_rows(start, d):
        return pl.ds(pl.multiple_of(start + lax.rem(z + d, NZ) * own, own), own)

    def all_sent(sem, ref):
        remote(ref, ref, sem, sem, row, col).wait_send()

    def all_here(sem, ref):
        remote(ref, ref, sem, sem, row, col).wait_recv()

    def x_peer(d):
        return lax.rem(x + d, NX) * 2 + core

    barrier = pltpu.get_barrier_semaphore()

    def greet(r, c):
        pl.semaphore_signal(barrier, inc=1, device_id=(r, c), device_id_type=MESH)

    for d in Z_ORDER:
        greet(z_peer(d), col)
    for d in (2, 1, 3):
        greet(row, x_peer(d))
    for d in range(1, NY):
        greet(y_peer(d), col)
    greet(row, other)

    chunk = depth // CHUNKS
    load_panel = pltpu.make_async_copy(panel_hbm, lf.at[:, col], load_s.at[0])
    load_rhs = pltpu.make_async_copy(rhs_hbm, rhs_v, load_s.at[1])
    loads_b = [
        pltpu.make_async_copy(
            b_hbm.at[chunk * k : chunk * (k + 1), :], b_v.at[chunk * k : chunk * (k + 1), :], load_b.at[k]
        )
        for k in range(CHUNKS)
    ]

    def load(n):
        return pltpu.make_async_copy(a_hbm.at[:, PIECE * n : PIECE * (n + 1)], a_v.at[n], load_a.at[n])

    load_panel.start()
    for copy in loads_b:
        copy.start()
    load(3).start()
    load_rhs.start()

    load_panel.wait()
    at = pl.multiple_of(x * SUB, SUB)
    tiles = [lf[m, col, :, pl.ds(at, SUB)].astype(F32) for m in (0, 1)]
    turned = [pltpu.roll(tile, slab, 1) for tile in tiles]
    even = core == 0
    block = jnp.concatenate([jnp.where(even, tiles[0], turned[0]), jnp.where(even, turned[1], tiles[1])], axis=0)
    inverse = unit_inverse(block)
    dall[col] = inverse[:slab] + inverse[slab:]

    for k in range(CHUNKS):
        loads_b[k].wait()
        bt[:, chunk * k : chunk * (k + 1)] = b_v[chunk * k : chunk * (k + 1), :].T

    load(2).start()

    pl.semaphore_wait(barrier, (NY - 1) + (NZ - 1) + (NX - 1) + 1)

    def part(p, c):
        return dall.at[c] if p == 0 else lf.at[(1, 0, 2)[p - 1], c]

    def along_x(p, d):
        return remote(part(p, col), part(p, col), px_s.at[p], px_r.at[p, d - 1], row, x_peer(d))

    def across(p, d):
        shard = part(p, lax.rem(x + NX - d, NX) * 2 + core)
        return remote(shard, shard, pc_s.at[p], pc_r.at[p], row, other)

    def send_panel(p):
        for d in (2, 1, 3):
            along_x(p, d).start()
        across(p, 0).start()

    send_panel(0)
    send_panel(1)

    place[...] = jnp.zeros_like(place)
    load_rhs.wait()
    place[pl.ds(pl.multiple_of(z * (PIECE // NZ), 8), PIECE // NZ), :] = rhs_v[...]

    def y_group(target):
        return pl.multiple_of(target // NZ * group, group)

    right_rows, left_rows = y_group(right), y_group(left)
    far_rows = pl.multiple_of(lax.rem(y + 2, NY) * group, group)
    own_rows = pl.multiple_of(y * group, group)

    def y_copy(n, slot):
        start = ((right_rows, 1), (far_rows, 0), (right_rows, 0), (left_rows, 0), (far_rows, 1), (left_rows, 1))[slot]
        src = ut.at[n, pl.ds(start[0] + start[1] * half, half), :]
        target = right if slot < 3 else left
        return remote(src, yrecv.at[n, Y_SLOT[slot]], y_s, y_r.at[n, Y_SEM[slot]], target, col)

    def y_start(n, slots):
        for slot in slots:
            y_copy(n, slot).start()

    def update(n):
        load(n).wait()
        if n >= 2:
            load(n - 2).start()
        ut[n] = mm(bt[...], a_v[n])

        @pl.when(n == y)
        def _():
            ut[n] = ut[n] - place[...].T

    def relay(n):
        all_here(y_r.at[n, 0], yrecv.at[n, 0])
        ut[n, pl.ds(right_rows, half), :] += yrecv[n, 0]
        y_copy(n, 2).start()
        all_here(y_r.at[n, 1], yrecv.at[n, 1])
        ut[n, pl.ds(left_rows + half, half), :] += yrecv[n, 1]
        y_copy(n, 5).start()

    def z_copy(n, d):
        return remote(w.at[n, z_rows(0, d), :], zrecv.at[n, d - 1], z_s, z_r.at[n], z_peer(d), col)

    def y_sum(n):
        all_here(y_r.at[n, 2], yrecv.at[n, 2:6])
        w[n, :half, :] = ut[n, pl.ds(own_rows, half), :] + (yrecv[n, 3] + yrecv[n, 4])
        w[n, half:, :] = ut[n, pl.ds(own_rows + half, half), :] + (yrecv[n, 2] + yrecv[n, 5])
        for d in Z_ORDER:
            z_copy(n, d).start()

    def forward(p):
        for d in range(1, NX):
            along_x(p, d).wait_recv()
            across(p, d).start()

    def arrived(p):
        all_here(pc_r.at[p], dall.at[0:NX] if p == 0 else lf.at[0, 0:NX])

    update(3)
    y_start(3, (1, 4))
    update(2)
    y_start(2, (1, 4))
    y_start(3, (0, 3))
    update(1)
    y_start(1, (1, 4))
    relay(3)
    y_start(2, (0, 3))
    update(0)
    y_start(0, (1, 4))
    relay(2)
    y_start(1, (0, 3))
    send_panel(2)
    relay(1)
    y_start(0, (0, 3))
    forward(0)
    forward(1)
    y_sum(3)
    relay(0)
    send_panel(3)
    y_sum(2)
    y_sum(1)

    def whole_inverse(m):
        lane = lax.broadcasted_iota(jnp.int32, (slab, SUB), 1)

        def small(i):
            first, second = dall[2 * i], dall[2 * i + 1]
            if m == 0:
                second = pltpu.roll(second, slab, 1)
            else:
                first = pltpu.roll(first, slab, 1)
            first = jnp.where(lane < slab, first, 0.0)
            second = jnp.where(lane < slab, 0.0, second)
            value = jnp.concatenate([first, second], axis=0)
            diagonal = lower(i, i)
            below = jnp.where(within(slab), diagonal, jnp.zeros_like(diagonal))
            return value - mm_split(mm_exact(value, below), value)

        def lower(i, j):
            return lf[m, 2 * i : 2 * i + 2, :, SUB * j : SUB * (j + 1)].reshape(SUB, SUB)

        def pair(i):
            first, second = small(i), small(i + 1)
            below = -mm_split(mm_exact(second, lower(i + 1, i)), first)
            top = jnp.concatenate([first, jnp.zeros_like(first)], axis=1)
            return jnp.concatenate([top, jnp.concatenate([below, second], axis=1)], axis=0)

        first, second = pair(0), pair(2)
        off = lf[m, 4:, :, : 2 * SUB].reshape(2 * SUB, 2 * SUB)
        below = -mm_split(mm_exact(second, off), first)
        for rows, columns, value in (
            (slice(0, 2 * SUB), slice(0, 2 * SUB), first),
            (slice(0, 2 * SUB), slice(2 * SUB, BLOCK), jnp.zeros_like(first)),
            (slice(2 * SUB, BLOCK), slice(0, 2 * SUB), below),
            (slice(2 * SUB, BLOCK), slice(2 * SUB, BLOCK), second),
        ):
            high, low = split(value)
            mh[m, rows, columns] = high
            ml[m, rows, columns] = low

    def reduced(h):
        pieces = []
        for n in (2 * h, 2 * h + 1):
            all_here(z_r.at[n], zrecv.at[n])
            total = w[n, z_rows(0, 0), :]
            for d in range(1, NZ):
                total = total + zrecv[n, d - 1]
            pieces.append(-total)
        return jnp.concatenate(pieces, axis=1)

    def solve(h, value):
        return stacked(value, mh[h]) + mm(value.astype(BF16), ml[h])

    def gz_copy(h, d):
        rows = g.at[h, z_rows(own_rows, 0), :]
        return remote(rows, rows, gz_s, gz_r.at[h, 0 if d in NEAR else 1], z_peer(d), col)

    def gy_copy(h, d, start, columns, sem, side):
        rows = g.at[h, z_rows(start, d), columns]
        return remote(rows, rows, gy_s, gy_r.at[h, sem], y_peer(side), col)

    def spread(h, distances, wave):
        for d in distances:
            gy_copy(h, d, own_rows, WHOLE, wave, 1).start()
            gy_copy(h, d, own_rows, WHOLE, 3 + wave, 3).start()

    def pass_on(h, distances, wave):
        size = g.at[h, 0 : len(distances) * own, :]
        all_here(gy_r.at[h, wave], size)
        for d in distances:
            gy_copy(h, d, left_rows, FRONT, 6, 1).start()
        all_here(gy_r.at[h, 3 + wave], size)
        for d in distances:
            gy_copy(h, d, right_rows, BACK, 6, 3).start()

    def publish(h, value):
        g[h, z_rows(own_rows, 0), :] = value
        for d in Z_ORDER:
            gz_copy(h, d).start()
        spread(h, (0,), 0)

    def spread_near(h):
        all_here(gz_r.at[h, 0], g.at[h, 0 : 4 * own, :])
        spread(h, NEAR, 1)

    def spread_far(h):
        all_here(gz_r.at[h, 1], g.at[h, 0 : 3 * own, :])
        if h == 0:
            for d in FAR:
                gy_copy(h, d, own_rows, WHOLE, 6, 2).start()
        spread(h, FAR, 2)

    def finish(h):
        if h == 0:
            all_here(gy_r.at[h, 2], g.at[h, 0 : 3 * own, :])
            all_here(gy_r.at[h, 5], g.at[h, 0 : 3 * own, :])
        all_here(gy_r.at[h, 6], g.at[h, 0:group, :])
        out_ref[h * BLOCK : (h + 1) * BLOCK, :] = g[h].T

    arrived(0)
    arrived(1)
    whole_inverse(1)
    y_sum(0)
    forward(2)
    second = solve(1, reduced(1))
    publish(1, second)
    forward(3)
    arrived(2)
    whole_inverse(0)
    arrived(3)
    coupled = stacked(second, lf[2].reshape(BLOCK, BLOCK))
    first = solve(0, reduced(0) - coupled)
    publish(0, first)
    pass_on(1, (0,), 0)
    spread_near(1)
    spread_far(1)
    spread_near(0)
    pass_on(1, NEAR, 1)
    pass_on(0, (0,), 0)
    spread_far(0)
    pass_on(1, FAR, 2)
    all_sent(y_s, yrecv)
    all_sent(z_s, zrecv)
    for p in range(PARTS):
        across_size = dall.at[0:NX] if p == 0 else lf.at[0, 0:NX]
        along_size = dall.at[0 : NX - 1] if p == 0 else lf.at[0, 0 : NX - 1]
        all_sent(px_s.at[p], along_size)
        all_sent(pc_s.at[p], across_size)
    pass_on(0, NEAR, 1)
    finish(1)
    all_sent(gz_s, g.at[:, 0 : 7 * own, :])
    finish(0)
    all_sent(gy_s, g.at[:, 0 : 3 * group, :])


def shards(tail_factor, tail_solution, panel_rhs, panel_factor):
    depth, window = tail_factor.shape
    width = tail_solution.shape[1]
    group, own = width // NY, width // (NY * NZ)
    slab = panel_factor.shape[1]
    dma = pltpu.SemaphoreType.DMA
    scratch = [
        pltpu.VMEM((PIECES, depth, PIECE), BF16),
        pltpu.VMEM((depth, width), BF16),
        pltpu.VMEM((width, depth), BF16),
        pltpu.VMEM(panel_rhs.shape, F32),
        pltpu.VMEM((PIECE, width), F32),
        pltpu.VMEM((PIECES, width, PIECE), F32),
        pltpu.VMEM((PIECES, 6, group // 2, PIECE), F32),
        pltpu.VMEM((PIECES, group, PIECE), F32),
        pltpu.VMEM((PIECES, NZ - 1, own, PIECE), F32),
        pltpu.VMEM((2, width, BLOCK), F32),
        pltpu.VMEM((3, 2 * NX, slab, BLOCK), BF16),
        pltpu.VMEM((2 * NX, slab, SUB), F32),
        pltpu.VMEM((2, BLOCK, BLOCK), BF16),
        pltpu.VMEM((2, BLOCK, BLOCK), BF16),
        dma((CHUNKS,)), dma((PIECES,)), dma((2,)),
        dma, dma((PIECES, 3)),
        dma, dma((PIECES,)),
        dma, dma((2, 2)),
        dma, dma((2, 7)),
        dma((PARTS,)), dma((PARTS, NX - 1)),
        dma((PARTS,)), dma((PARTS,)),
    ]
    return pl.pallas_call(
        kernel,
        out_shape=jax.ShapeDtypeStruct((window, width), F32),
        in_specs=[pl.BlockSpec(memory_space=pltpu.HBM)] * 4,
        out_specs=pl.BlockSpec(memory_space=pltpu.VMEM),
        scratch_shapes=scratch,
        compiler_params=pltpu.CompilerParams(
            collective_id=0, has_side_effects=True, vmem_limit_bytes=52 * 1024 * 1024
        ),
    )(tail_factor, tail_solution, pltpu.with_memory_space_constraint(panel_rhs, pltpu.HBM), pltpu.with_memory_space_constraint(panel_factor, pltpu.HBM))


def solution(mesh):
    return jax.shard_map(
        shards,
        mesh=mesh,
        in_specs=(P("row", None), P("row", "col"), P("row", "col"), P(None, "col", None)),
        out_specs=P(None, "col"),
        check_vma=False,
    )
```

```python
import jax
import jax.numpy as jnp
from jax import lax
from jax.experimental import pallas as pl
from jax.experimental.pallas import tpu as pltpu
from jax.sharding import PartitionSpec as P

MESH = pl.DeviceIdType.MESH
F32 = jnp.float32
BF16 = jnp.bfloat16

NY, NZ, NX = 4, 8, 4
BLOCK = 512
WINDOW = 2 * BLOCK
PIECE = 256
PIECES = WINDOW // PIECE
SUB = 128
CHUNKS = 4
NEAR, FAR = (1, 7, 2, 6), (3, 5, 4)
Z_ORDER = (4, 3, 5, 2, 6, 1, 7)
WHOLE, FRONT, BACK = slice(0, BLOCK), slice(0, BLOCK // 2), slice(BLOCK // 2, BLOCK)
Y_SLOT = (2, 0, 3, 4, 1, 5)
Y_SEM = (2, 0, 2, 2, 1, 2)
PARTS = 4


def split(x):
    high = x.astype(BF16)
    return high, (x - high.astype(F32)).astype(BF16)


def mm(a, b):
    return jnp.dot(a, b, preferred_element_type=F32)


def mm_exact(a, b):
    high, low = split(a)
    return mm(high, b) + mm(low, b)


def mm_split(a, b):
    a_high, a_low = split(a)
    b_high, b_low = split(b)
    return mm(a_high, b_high) + (mm(a_low, b_high) + mm(a_high, b_low))


def stacked(a, b):
    rows = a.shape[0]
    both = mm(jnp.concatenate(split(a), axis=0), b)
    return both[:rows] + both[rows:]


def within(size):
    row = lax.broadcasted_iota(jnp.int32, (SUB, SUB), 0)
    col = lax.broadcasted_iota(jnp.int32, (SUB, SUB), 1)
    return (row // (2 * size) == col // (2 * size)) & (row // size == col // size + 1)


def unit_inverse(block):
    row = lax.broadcasted_iota(jnp.int32, (SUB, SUB), 0)
    col = lax.broadcasted_iota(jnp.int32, (SUB, SUB), 1)
    inverse = jnp.where(row == col, 1.0, 0.0) - jnp.where(within(1), block, 0.0)
    size = 2
    while size < SUB // 2:
        below = jnp.where(within(size), block, 0.0).astype(BF16)
        inverse = inverse - mm_split(mm_exact(inverse, below), inverse)
        size *= 2
    return inverse


def kernel(
    a_hbm, b_hbm, rhs_hbm, panel_hbm, out_ref,
    a_v, b_v, bt, rhs_v, place, ut, yrecv, w, zrecv, g, lf, dall, mh, ml,
    load_b, load_a, load_s, y_s, y_r, z_s, z_r, gz_s, gz_r, gy_s, gy_r, px_s, px_r, pc_s, pc_r,
):
    row, col = lax.axis_index("row"), lax.axis_index("col")
    y, z = row // NZ, row % NZ
    x, core = col // 2, col % 2
    other = x * 2 + (1 - core)
    right = lax.rem(y + 1, NY) * NZ + z
    left = lax.rem(y + NY - 1, NY) * NZ + z
    depth, width = b_hbm.shape
    group = width // NY
    half = group // 2
    own = width // (NY * NZ)
    slab = panel_hbm.shape[1]

    def remote(src, dst, send, recv, r, c):
        return pltpu.make_async_remote_copy(
            src_ref=src, dst_ref=dst, send_sem=send, recv_sem=recv,
            device_id=(r, c), device_id_type=MESH,
        )

    def z_peer(d):
        return y * NZ + lax.rem(z + d, NZ)

    def y_peer(d):
        return lax.rem(y + d, NY) * NZ + z

    def z_rows(start, d):
        return pl.ds(pl.multiple_of(start + lax.rem(z + d, NZ) * own, own), own)

    def all_sent(sem, ref):
        remote(ref, ref, sem, sem, row, col).wait_send()

    def all_here(sem, ref):
        remote(ref, ref, sem, sem, row, col).wait_recv()

    def x_peer(d):
        return lax.rem(x + d, NX) * 2 + core

    barrier = pltpu.get_barrier_semaphore()

    def greet(r, c):
        pl.semaphore_signal(barrier, inc=1, device_id=(r, c), device_id_type=MESH)

    for d in Z_ORDER:
        greet(z_peer(d), col)
    for d in (2, 1, 3):
        greet(row, x_peer(d))
    for d in range(1, NY):
        greet(y_peer(d), col)
    greet(row, other)

    chunk = depth // CHUNKS
    load_panel = pltpu.make_async_copy(panel_hbm, lf.at[:, col], load_s.at[0])
    load_rhs = pltpu.make_async_copy(rhs_hbm, rhs_v, load_s.at[1])
    loads_b = [
        pltpu.make_async_copy(
            b_hbm.at[chunk * k : chunk * (k + 1), :], b_v.at[chunk * k : chunk * (k + 1), :], load_b.at[k]
        )
        for k in range(CHUNKS)
    ]

    def load(n):
        return pltpu.make_async_copy(a_hbm.at[:, PIECE * n : PIECE * (n + 1)], a_v.at[n], load_a.at[n])

    load_rhs.start()
    for copy in loads_b:
        copy.start()
    load(3).start()
    load_panel.start()

    for k in range(CHUNKS):
        loads_b[k].wait()
        bt[:, chunk * k : chunk * (k + 1)] = b_v[chunk * k : chunk * (k + 1), :].T

    load(2).start()


    def part(p, c):
        return dall.at[c] if p == 0 else lf.at[(1, 0, 2)[p - 1], c]

    def along_x(p, d):
        return remote(part(p, col), part(p, col), px_s.at[p], px_r.at[p, d - 1], row, x_peer(d))

    def across(p, d):
        shard = part(p, lax.rem(x + NX - d, NX) * 2 + core)
        return remote(shard, shard, pc_s.at[p], pc_r.at[p], row, other)

    def send_panel(p):
        for d in (2, 1, 3):
            along_x(p, d).start()
        across(p, 0).start()

    place[...] = jnp.zeros_like(place)
    load_rhs.wait()
    place[pl.ds(pl.multiple_of(z * (PIECE // NZ), 8), PIECE // NZ), :] = rhs_v[...]

    def y_group(target):
        return pl.multiple_of(target // NZ * group, group)

    right_rows, left_rows = y_group(right), y_group(left)
    far_rows = pl.multiple_of(lax.rem(y + 2, NY) * group, group)
    own_rows = pl.multiple_of(y * group, group)

    def y_copy(n, slot):
        start = ((right_rows, 1), (far_rows, 0), (right_rows, 0), (left_rows, 0), (far_rows, 1), (left_rows, 1))[slot]
        src = ut.at[n, pl.ds(start[0] + start[1] * half, half), :]
        target = right if slot < 3 else left
        return remote(src, yrecv.at[n, Y_SLOT[slot]], y_s, y_r.at[n, Y_SEM[slot]], target, col)

    def y_start(n, slots):
        for slot in slots:
            y_copy(n, slot).start()

    def update(n):
        load(n).wait()
        if n >= 2:
            load(n - 2).start()
        ut[n] = mm(bt[...], a_v[n])

        @pl.when(n == y)
        def _():
            ut[n] = ut[n] - place[...].T

    def relay(n):
        all_here(y_r.at[n, 0], yrecv.at[n, 0])
        ut[n, pl.ds(right_rows, half), :] += yrecv[n, 0]
        y_copy(n, 2).start()
        all_here(y_r.at[n, 1], yrecv.at[n, 1])
        ut[n, pl.ds(left_rows + half, half), :] += yrecv[n, 1]
        y_copy(n, 5).start()

    def z_copy(n, d):
        return remote(w.at[n, z_rows(0, d), :], zrecv.at[n, d - 1], z_s, z_r.at[n], z_peer(d), col)

    def y_sum(n):
        all_here(y_r.at[n, 2], yrecv.at[n, 2:6])
        w[n, :half, :] = ut[n, pl.ds(own_rows, half), :] + (yrecv[n, 3] + yrecv[n, 4])
        w[n, half:, :] = ut[n, pl.ds(own_rows + half, half), :] + (yrecv[n, 2] + yrecv[n, 5])
        for d in Z_ORDER:
            z_copy(n, d).start()

    def forward(p):
        for d in range(1, NX):
            along_x(p, d).wait_recv()
            across(p, d).start()

    def arrived(p):
        all_here(pc_r.at[p], dall.at[0:NX] if p == 0 else lf.at[0, 0:NX])

    update(3)
    pl.semaphore_wait(barrier, (NY - 1) + (NZ - 1) + (NX - 1) + 1)
    y_start(3, (1, 4))
    load_panel.wait()
    send_panel(1)
    update(2)
    y_start(2, (1, 4))
    y_start(3, (0, 3))
    update(1)
    y_start(1, (1, 4))
    at = pl.multiple_of(x * SUB, SUB)
    tiles = [lf[m, col, :, pl.ds(at, SUB)].astype(F32) for m in (0, 1)]
    turned = [pltpu.roll(tile, slab, 1) for tile in tiles]
    even = core == 0
    block = jnp.concatenate([jnp.where(even, tiles[0], turned[0]), jnp.where(even, turned[1], tiles[1])], axis=0)
    inverse = unit_inverse(block)
    dall[col] = inverse[:slab] + inverse[slab:]
    send_panel(0)
    relay(3)
    y_start(2, (0, 3))
    update(0)
    y_start(0, (1, 4))
    relay(2)
    y_start(1, (0, 3))
    send_panel(2)
    relay(1)
    y_start(0, (0, 3))
    forward(1)
    y_sum(3)
    relay(0)
    forward(0)
    send_panel(3)
    y_sum(2)
    y_sum(1)

    def whole_inverse(m):
        lane = lax.broadcasted_iota(jnp.int32, (slab, SUB), 1)

        def small(i):
            first, second = dall[2 * i], dall[2 * i + 1]
            if m == 0:
                second = pltpu.roll(second, slab, 1)
            else:
                first = pltpu.roll(first, slab, 1)
            first = jnp.where(lane < slab, first, 0.0)
            second = jnp.where(lane < slab, 0.0, second)
            value = jnp.concatenate([first, second], axis=0)
            diagonal = lower(i, i)
            below = jnp.where(within(slab), diagonal, jnp.zeros_like(diagonal))
            return value - mm_split(mm_exact(value, below), value)

        def lower(i, j):
            return lf[m, 2 * i : 2 * i + 2, :, SUB * j : SUB * (j + 1)].reshape(SUB, SUB)

        def pair(i):
            first, second = small(i), small(i + 1)
            below = -mm_split(mm_exact(second, lower(i + 1, i)), first)
            top = jnp.concatenate([first, jnp.zeros_like(first)], axis=1)
            return jnp.concatenate([top, jnp.concatenate([below, second], axis=1)], axis=0)

        first, second = pair(0), pair(2)
        off = lf[m, 4:, :, : 2 * SUB].reshape(2 * SUB, 2 * SUB)
        below = -mm_split(mm_exact(second, off), first)
        for rows, columns, value in (
            (slice(0, 2 * SUB), slice(0, 2 * SUB), first),
            (slice(0, 2 * SUB), slice(2 * SUB, BLOCK), jnp.zeros_like(first)),
            (slice(2 * SUB, BLOCK), slice(0, 2 * SUB), below),
            (slice(2 * SUB, BLOCK), slice(2 * SUB, BLOCK), second),
        ):
            high, low = split(value)
            mh[m, rows, columns] = high
            ml[m, rows, columns] = low

    def reduced(h):
        pieces = []
        for n in (2 * h, 2 * h + 1):
            all_here(z_r.at[n], zrecv.at[n])
            total = w[n, z_rows(0, 0), :]
            for d in range(1, NZ):
                total = total + zrecv[n, d - 1]
            pieces.append(-total)
        return jnp.concatenate(pieces, axis=1)

    def solve(h, value):
        return stacked(value, mh[h]) + mm(value.astype(BF16), ml[h])

    def gz_copy(h, d):
        rows = g.at[h, z_rows(own_rows, 0), :]
        return remote(rows, rows, gz_s, gz_r.at[h, 0 if d in NEAR else 1], z_peer(d), col)

    def gy_copy(h, d, start, columns, sem, side):
        rows = g.at[h, z_rows(start, d), columns]
        return remote(rows, rows, gy_s, gy_r.at[h, sem], y_peer(side), col)

    def spread(h, distances, wave):
        for d in distances:
            gy_copy(h, d, own_rows, WHOLE, wave, 1).start()
            gy_copy(h, d, own_rows, WHOLE, 3 + wave, 3).start()

    def pass_on(h, distances, wave):
        size = g.at[h, 0 : len(distances) * own, :]
        all_here(gy_r.at[h, wave], size)
        for d in distances:
            gy_copy(h, d, left_rows, FRONT, 6, 1).start()
        all_here(gy_r.at[h, 3 + wave], size)
        for d in distances:
            gy_copy(h, d, right_rows, BACK, 6, 3).start()

    def publish(h, value):
        g[h, z_rows(own_rows, 0), :] = value
        for d in Z_ORDER:
            gz_copy(h, d).start()
        spread(h, (0,), 0)

    def spread_near(h):
        all_here(gz_r.at[h, 0], g.at[h, 0 : 4 * own, :])
        spread(h, NEAR, 1)

    def spread_far(h):
        all_here(gz_r.at[h, 1], g.at[h, 0 : 3 * own, :])
        if h == 0:
            for d in FAR:
                gy_copy(h, d, own_rows, WHOLE, 6, 2).start()
        spread(h, FAR, 2)

    def finish(h):
        if h == 0:
            all_here(gy_r.at[h, 2], g.at[h, 0 : 3 * own, :])
            all_here(gy_r.at[h, 5], g.at[h, 0 : 3 * own, :])
        all_here(gy_r.at[h, 6], g.at[h, 0:group, :])
        out_ref[h * BLOCK : (h + 1) * BLOCK, :] = g[h].T

    arrived(0)
    arrived(1)
    whole_inverse(1)
    y_sum(0)
    forward(2)
    second = solve(1, reduced(1))
    publish(1, second)
    forward(3)
    arrived(2)
    whole_inverse(0)
    arrived(3)
    coupled = stacked(second, lf[2].reshape(BLOCK, BLOCK))
    first = solve(0, reduced(0) - coupled)
    publish(0, first)
    pass_on(1, (0,), 0)
    spread_near(1)
    spread_far(1)
    spread_near(0)
    pass_on(1, NEAR, 1)
    pass_on(0, (0,), 0)
    spread_far(0)
    pass_on(1, FAR, 2)
    all_sent(y_s, yrecv)
    all_sent(z_s, zrecv)
    for p in range(PARTS):
        across_size = dall.at[0:NX] if p == 0 else lf.at[0, 0:NX]
        along_size = dall.at[0 : NX - 1] if p == 0 else lf.at[0, 0 : NX - 1]
        all_sent(px_s.at[p], along_size)
        all_sent(pc_s.at[p], across_size)
    pass_on(0, NEAR, 1)
    finish(1)
    all_sent(gz_s, g.at[:, 0 : 7 * own, :])
    finish(0)
    all_sent(gy_s, g.at[:, 0 : 3 * group, :])


def shards(tail_factor, tail_solution, panel_rhs, panel_factor):
    depth, window = tail_factor.shape
    width = tail_solution.shape[1]
    group, own = width // NY, width // (NY * NZ)
    slab = panel_factor.shape[1]
    dma = pltpu.SemaphoreType.DMA
    scratch = [
        pltpu.VMEM((PIECES, depth, PIECE), BF16),
        pltpu.VMEM((depth, width), BF16),
        pltpu.VMEM((width, depth), BF16),
        pltpu.VMEM(panel_rhs.shape, F32),
        pltpu.VMEM((PIECE, width), F32),
        pltpu.VMEM((PIECES, width, PIECE), F32),
        pltpu.VMEM((PIECES, 6, group // 2, PIECE), F32),
        pltpu.VMEM((PIECES, group, PIECE), F32),
        pltpu.VMEM((PIECES, NZ - 1, own, PIECE), F32),
        pltpu.VMEM((2, width, BLOCK), F32),
        pltpu.VMEM((3, 2 * NX, slab, BLOCK), BF16),
        pltpu.VMEM((2 * NX, slab, SUB), F32),
        pltpu.VMEM((2, BLOCK, BLOCK), BF16),
        pltpu.VMEM((2, BLOCK, BLOCK), BF16),
        dma((CHUNKS,)), dma((PIECES,)), dma((2,)),
        dma, dma((PIECES, 3)),
        dma, dma((PIECES,)),
        dma, dma((2, 2)),
        dma, dma((2, 7)),
        dma((PARTS,)), dma((PARTS, NX - 1)),
        dma((PARTS,)), dma((PARTS,)),
    ]
    return pl.pallas_call(
        kernel,
        out_shape=jax.ShapeDtypeStruct((window, width), F32),
        in_specs=[pl.BlockSpec(memory_space=pltpu.HBM)] * 4,
        out_specs=pl.BlockSpec(memory_space=pltpu.VMEM),
        scratch_shapes=scratch,
        compiler_params=pltpu.CompilerParams(
            collective_id=0, has_side_effects=True, vmem_limit_bytes=52 * 1024 * 1024
        ),
    )(tail_factor, tail_solution, pltpu.with_memory_space_constraint(panel_rhs, pltpu.HBM), pltpu.with_memory_space_constraint(panel_factor, pltpu.HBM))


def solution(mesh):
    return jax.shard_map(
        shards,
        mesh=mesh,
        in_specs=(P("row", None), P("row", "col"), P("row", "col"), P(None, "col", None)),
        out_specs=P(None, "col"),
        check_vma=False,
    )
```

```python
import jax
import jax.numpy as jnp
from jax import lax
from jax.experimental import pallas as pl
from jax.experimental.pallas import tpu as pltpu
from jax.sharding import PartitionSpec as P

MESH = pl.DeviceIdType.MESH
F32 = jnp.float32
BF16 = jnp.bfloat16

NY, NZ, NX = 4, 8, 4
BLOCK = 512
WINDOW = 2 * BLOCK
PIECE = 256
PIECES = WINDOW // PIECE
SUB = 128
CHUNKS = 4
NEAR, FAR = (1, 7, 2, 6), (3, 5, 4)
Z_ORDER = (4, 3, 5, 2, 6, 1, 7)
WHOLE, FRONT, BACK = slice(0, BLOCK), slice(0, BLOCK // 2), slice(BLOCK // 2, BLOCK)
Y_SLOT = (2, 0, 3, 4, 1, 5)
Y_SEM = (2, 0, 2, 2, 1, 2)
PARTS = 4


def split(x):
    high = x.astype(BF16)
    return high, (x - high.astype(F32)).astype(BF16)


def mm(a, b):
    return jnp.dot(a, b, preferred_element_type=F32)


def mm_exact(a, b):
    high, low = split(a)
    return mm(high, b) + mm(low, b)


def mm_split(a, b):
    a_high, a_low = split(a)
    b_high, b_low = split(b)
    return mm(a_high, b_high) + (mm(a_low, b_high) + mm(a_high, b_low))


def stacked(a, b):
    rows = a.shape[0]
    both = mm(jnp.concatenate(split(a), axis=0), b)
    return both[:rows] + both[rows:]


def within(size):
    row = lax.broadcasted_iota(jnp.int32, (SUB, SUB), 0)
    col = lax.broadcasted_iota(jnp.int32, (SUB, SUB), 1)
    return (row // (2 * size) == col // (2 * size)) & (row // size == col // size + 1)


def unit_inverse(block):
    row = lax.broadcasted_iota(jnp.int32, (SUB, SUB), 0)
    col = lax.broadcasted_iota(jnp.int32, (SUB, SUB), 1)
    inverse = jnp.where(row == col, 1.0, 0.0) - jnp.where(within(1), block, 0.0)
    size = 2
    while size < SUB // 2:
        below = jnp.where(within(size), block, 0.0).astype(BF16)
        inverse = inverse - mm_split(mm_exact(inverse, below), inverse)
        size *= 2
    return inverse


def kernel(
    a_hbm, b_hbm, rhs_hbm, panel_hbm, out_ref,
    a_v, b_v, bt, rhs_v, place, ut, yrecv, w, zrecv, g, lf, dall, mh, ml,
    load_b, load_a, load_s, y_s, y_r, z_s, z_r, gz_s, gz_r, gy_s, gy_r, px_s, px_r, pc_s, pc_r,
):
    row, col = lax.axis_index("row"), lax.axis_index("col")
    y, z = row // NZ, row % NZ
    x, core = col // 2, col % 2
    other = x * 2 + (1 - core)
    right = lax.rem(y + 1, NY) * NZ + z
    left = lax.rem(y + NY - 1, NY) * NZ + z
    depth, width = b_hbm.shape
    group = width // NY
    half = group // 2
    own = width // (NY * NZ)
    slab = panel_hbm.shape[1]

    def remote(src, dst, send, recv, r, c):
        return pltpu.make_async_remote_copy(
            src_ref=src, dst_ref=dst, send_sem=send, recv_sem=recv,
            device_id=(r, c), device_id_type=MESH,
        )

    def z_peer(d):
        return y * NZ + lax.rem(z + d, NZ)

    def y_peer(d):
        return lax.rem(y + d, NY) * NZ + z

    def z_rows(start, d):
        return pl.ds(pl.multiple_of(start + lax.rem(z + d, NZ) * own, own), own)

    def all_sent(sem, ref):
        remote(ref, ref, sem, sem, row, col).wait_send()

    def all_here(sem, ref):
        remote(ref, ref, sem, sem, row, col).wait_recv()

    def x_peer(d):
        return lax.rem(x + d, NX) * 2 + core

    barrier = pltpu.get_barrier_semaphore()

    def greet(r, c):
        pl.semaphore_signal(barrier, inc=1, device_id=(r, c), device_id_type=MESH)

    for d in Z_ORDER:
        greet(z_peer(d), col)
    for d in (2, 1, 3):
        greet(row, x_peer(d))
    for d in range(1, NY):
        greet(y_peer(d), col)
    greet(row, other)

    chunk = depth // CHUNKS
    load_panel = pltpu.make_async_copy(panel_hbm, lf.at[:, col], load_s.at[0])
    load_rhs = pltpu.make_async_copy(rhs_hbm, rhs_v, load_s.at[1])
    loads_b = [
        pltpu.make_async_copy(
            b_hbm.at[chunk * k : chunk * (k + 1), :], b_v.at[chunk * k : chunk * (k + 1), :], load_b.at[k]
        )
        for k in range(CHUNKS)
    ]

    def load(n):
        return pltpu.make_async_copy(a_hbm.at[:, PIECE * n : PIECE * (n + 1)], a_v.at[n], load_a.at[n])

    load_rhs.start()
    for copy in loads_b:
        copy.start()
    load(3).start()
    load_panel.start()

    for k in range(CHUNKS):
        loads_b[k].wait()
        bt[:, chunk * k : chunk * (k + 1)] = b_v[chunk * k : chunk * (k + 1), :].T

    load(2).start()


    def part(p, c):
        return dall.at[c] if p == 0 else lf.at[(1, 0, 2)[p - 1], c]

    def along_x(p, d):
        return remote(part(p, col), part(p, col), px_s.at[p], px_r.at[p, d - 1], row, x_peer(d))

    def across(p, d):
        shard = part(p, lax.rem(x + NX - d, NX) * 2 + core)
        return remote(shard, shard, pc_s.at[p], pc_r.at[p], row, other)

    def send_panel(p):
        for d in (2, 1, 3):
            along_x(p, d).start()
        across(p, 0).start()

    place[...] = jnp.zeros_like(place)
    load_rhs.wait()
    place[pl.ds(pl.multiple_of(z * (PIECE // NZ), 8), PIECE // NZ), :] = rhs_v[...]

    def y_group(target):
        return pl.multiple_of(target // NZ * group, group)

    right_rows, left_rows = y_group(right), y_group(left)
    far_rows = pl.multiple_of(lax.rem(y + 2, NY) * group, group)
    own_rows = pl.multiple_of(y * group, group)

    def y_copy(n, slot):
        start = ((right_rows, 1), (far_rows, 0), (right_rows, 0), (left_rows, 0), (far_rows, 1), (left_rows, 1))[slot]
        src = ut.at[n, pl.ds(start[0] + start[1] * half, half), :]
        target = right if slot < 3 else left
        return remote(src, yrecv.at[n, Y_SLOT[slot]], y_s, y_r.at[n, Y_SEM[slot]], target, col)

    def y_start(n, slots):
        for slot in slots:
            y_copy(n, slot).start()

    def update(n):
        load(n).wait()
        if n >= 2:
            load(n - 2).start()
        ut[n] = mm(bt[...], a_v[n])

        @pl.when(n == y)
        def _():
            ut[n] = ut[n] - place[...].T

    def relay(n):
        all_here(y_r.at[n, 0], yrecv.at[n, 0])
        ut[n, pl.ds(right_rows, half), :] += yrecv[n, 0]
        y_copy(n, 2).start()
        all_here(y_r.at[n, 1], yrecv.at[n, 1])
        ut[n, pl.ds(left_rows + half, half), :] += yrecv[n, 1]
        y_copy(n, 5).start()

    def z_copy(n, d):
        return remote(w.at[n, z_rows(0, d), :], zrecv.at[n, d - 1], z_s, z_r.at[n], z_peer(d), col)

    def y_sum(n):
        all_here(y_r.at[n, 2], yrecv.at[n, 2:6])
        w[n, :half, :] = ut[n, pl.ds(own_rows, half), :] + (yrecv[n, 3] + yrecv[n, 4])
        w[n, half:, :] = ut[n, pl.ds(own_rows + half, half), :] + (yrecv[n, 2] + yrecv[n, 5])
        for d in Z_ORDER:
            z_copy(n, d).start()

    def forward(p):
        for d in range(1, NX):
            along_x(p, d).wait_recv()
            across(p, d).start()

    def arrived(p):
        all_here(pc_r.at[p], dall.at[0:NX] if p == 0 else lf.at[0, 0:NX])

    update(3)
    pl.semaphore_wait(barrier, (NY - 1) + (NZ - 1) + (NX - 1) + 1)
    y_start(3, (1, 4))
    load_panel.wait()
    send_panel(1)
    update(2)
    y_start(2, (1, 4))
    y_start(3, (0, 3))
    update(1)
    y_start(1, (1, 4))
    at = pl.multiple_of(x * SUB, SUB)
    tiles = [lf[m, col, :, pl.ds(at, SUB)].astype(F32) for m in (0, 1)]
    turned = [pltpu.roll(tile, slab, 1) for tile in tiles]
    even = core == 0
    block = jnp.concatenate([jnp.where(even, tiles[0], turned[0]), jnp.where(even, turned[1], tiles[1])], axis=0)
    inverse = unit_inverse(block)
    dall[col] = inverse[:slab] + inverse[slab:]
    send_panel(0)
    relay(3)
    y_start(2, (0, 3))
    update(0)
    y_start(0, (1, 4))
    relay(2)
    y_start(1, (0, 3))
    send_panel(2)
    relay(1)
    y_start(0, (0, 3))
    forward(1)
    y_sum(3)
    relay(0)
    forward(0)
    send_panel(3)
    y_sum(2)
    y_sum(1)
    forward(2)

    def whole_inverse(m):
        lane = lax.broadcasted_iota(jnp.int32, (slab, SUB), 1)

        def small(i):
            first, second = dall[2 * i], dall[2 * i + 1]
            if m == 0:
                second = pltpu.roll(second, slab, 1)
            else:
                first = pltpu.roll(first, slab, 1)
            first = jnp.where(lane < slab, first, 0.0)
            second = jnp.where(lane < slab, 0.0, second)
            value = jnp.concatenate([first, second], axis=0)
            diagonal = lower(i, i)
            below = jnp.where(within(slab), diagonal, jnp.zeros_like(diagonal))
            return value - mm_split(mm_exact(value, below), value)

        def lower(i, j):
            return lf[m, 2 * i : 2 * i + 2, :, SUB * j : SUB * (j + 1)].reshape(SUB, SUB)

        def pair(i):
            first, second = small(i), small(i + 1)
            below = -mm_split(mm_exact(second, lower(i + 1, i)), first)
            top = jnp.concatenate([first, jnp.zeros_like(first)], axis=1)
            return jnp.concatenate([top, jnp.concatenate([below, second], axis=1)], axis=0)

        first, second = pair(0), pair(2)
        off = lf[m, 4:, :, : 2 * SUB].reshape(2 * SUB, 2 * SUB)
        below = -mm_split(mm_exact(second, off), first)
        for rows, columns, value in (
            (slice(0, 2 * SUB), slice(0, 2 * SUB), first),
            (slice(0, 2 * SUB), slice(2 * SUB, BLOCK), jnp.zeros_like(first)),
            (slice(2 * SUB, BLOCK), slice(0, 2 * SUB), below),
            (slice(2 * SUB, BLOCK), slice(2 * SUB, BLOCK), second),
        ):
            high, low = split(value)
            mh[m, rows, columns] = high
            ml[m, rows, columns] = low

    def reduced(h):
        pieces = []
        for n in (2 * h, 2 * h + 1):
            all_here(z_r.at[n], zrecv.at[n])
            total = w[n, z_rows(0, 0), :]
            for d in range(1, NZ):
                total = total + zrecv[n, d - 1]
            pieces.append(-total)
        return jnp.concatenate(pieces, axis=1)

    def solve(h, value):
        return stacked(value, mh[h]) + mm(value.astype(BF16), ml[h])

    def gz_copy(h, d):
        rows = g.at[h, z_rows(own_rows, 0), :]
        return remote(rows, rows, gz_s, gz_r.at[h, 0 if d in NEAR else 1], z_peer(d), col)

    def gy_copy(h, d, start, columns, sem, side):
        rows = g.at[h, z_rows(start, d), columns]
        return remote(rows, rows, gy_s, gy_r.at[h, sem], y_peer(side), col)

    def spread(h, distances, wave):
        for d in distances:
            gy_copy(h, d, own_rows, WHOLE, wave, 1).start()
            gy_copy(h, d, own_rows, WHOLE, 3 + wave, 3).start()

    def pass_on(h, distances, wave):
        size = g.at[h, 0 : len(distances) * own, :]
        all_here(gy_r.at[h, wave], size)
        for d in distances:
            gy_copy(h, d, left_rows, FRONT, 6, 1).start()
        all_here(gy_r.at[h, 3 + wave], size)
        for d in distances:
            gy_copy(h, d, right_rows, BACK, 6, 3).start()

    def publish(h, value):
        g[h, z_rows(own_rows, 0), :] = value
        for d in Z_ORDER:
            gz_copy(h, d).start()
        spread(h, (0,), 0)

    def spread_near(h):
        all_here(gz_r.at[h, 0], g.at[h, 0 : 4 * own, :])
        spread(h, NEAR, 1)

    def spread_far(h):
        all_here(gz_r.at[h, 1], g.at[h, 0 : 3 * own, :])
        if h == 0:
            for d in FAR:
                gy_copy(h, d, own_rows, WHOLE, 6, 2).start()
        spread(h, FAR, 2)

    def finish(h):
        if h == 0:
            all_here(gy_r.at[h, 2], g.at[h, 0 : 3 * own, :])
            all_here(gy_r.at[h, 5], g.at[h, 0 : 3 * own, :])
        all_here(gy_r.at[h, 6], g.at[h, 0:group, :])
        out_ref[h * BLOCK : (h + 1) * BLOCK, :] = g[h].T

    arrived(0)
    arrived(1)
    whole_inverse(1)
    y_sum(0)
    second = solve(1, reduced(1))
    publish(1, second)
    forward(3)
    arrived(2)
    whole_inverse(0)
    arrived(3)
    coupled = stacked(second, lf[2].reshape(BLOCK, BLOCK))
    first = solve(0, reduced(0) - coupled)
    publish(0, first)
    pass_on(1, (0,), 0)
    spread_near(1)
    spread_far(1)
    spread_near(0)
    pass_on(1, NEAR, 1)
    pass_on(0, (0,), 0)
    spread_far(0)
    pass_on(1, FAR, 2)
    all_sent(y_s, yrecv)
    all_sent(z_s, zrecv)
    for p in range(PARTS):
        across_size = dall.at[0:NX] if p == 0 else lf.at[0, 0:NX]
        along_size = dall.at[0 : NX - 1] if p == 0 else lf.at[0, 0 : NX - 1]
        all_sent(px_s.at[p], along_size)
        all_sent(pc_s.at[p], across_size)
    pass_on(0, NEAR, 1)
    finish(1)
    all_sent(gz_s, g.at[:, 0 : 7 * own, :])
    finish(0)
    all_sent(gy_s, g.at[:, 0 : 3 * group, :])


def shards(tail_factor, tail_solution, panel_rhs, panel_factor):
    depth, window = tail_factor.shape
    width = tail_solution.shape[1]
    group, own = width // NY, width // (NY * NZ)
    slab = panel_factor.shape[1]
    dma = pltpu.SemaphoreType.DMA
    scratch = [
        pltpu.VMEM((PIECES, depth, PIECE), BF16),
        pltpu.VMEM((depth, width), BF16),
        pltpu.VMEM((width, depth), BF16),
        pltpu.VMEM(panel_rhs.shape, F32),
        pltpu.VMEM((PIECE, width), F32),
        pltpu.VMEM((PIECES, width, PIECE), F32),
        pltpu.VMEM((PIECES, 6, group // 2, PIECE), F32),
        pltpu.VMEM((PIECES, group, PIECE), F32),
        pltpu.VMEM((PIECES, NZ - 1, own, PIECE), F32),
        pltpu.VMEM((2, width, BLOCK), F32),
        pltpu.VMEM((3, 2 * NX, slab, BLOCK), BF16),
        pltpu.VMEM((2 * NX, slab, SUB), F32),
        pltpu.VMEM((2, BLOCK, BLOCK), BF16),
        pltpu.VMEM((2, BLOCK, BLOCK), BF16),
        dma((CHUNKS,)), dma((PIECES,)), dma((2,)),
        dma, dma((PIECES, 3)),
        dma, dma((PIECES,)),
        dma, dma((2, 2)),
        dma, dma((2, 7)),
        dma((PARTS,)), dma((PARTS, NX - 1)),
        dma((PARTS,)), dma((PARTS,)),
    ]
    return pl.pallas_call(
        kernel,
        out_shape=jax.ShapeDtypeStruct((window, width), F32),
        in_specs=[pl.BlockSpec(memory_space=pltpu.HBM)] * 4,
        out_specs=pl.BlockSpec(memory_space=pltpu.VMEM),
        scratch_shapes=scratch,
        compiler_params=pltpu.CompilerParams(
            collective_id=0, has_side_effects=True, vmem_limit_bytes=52 * 1024 * 1024
        ),
    )(tail_factor, tail_solution, pltpu.with_memory_space_constraint(panel_rhs, pltpu.HBM), pltpu.with_memory_space_constraint(panel_factor, pltpu.HBM))


def solution(mesh):
    return jax.shard_map(
        shards,
        mesh=mesh,
        in_specs=(P("row", None), P("row", "col"), P("row", "col"), P(None, "col", None)),
        out_specs=P(None, "col"),
        check_vma=False,
    )
```

```python
import jax
import jax.numpy as jnp
from jax import lax
from jax.experimental import pallas as pl
from jax.experimental.pallas import tpu as pltpu
from jax.sharding import PartitionSpec as P

MESH = pl.DeviceIdType.MESH
F32 = jnp.float32
BF16 = jnp.bfloat16

NY, NZ, NX = 4, 8, 4
BLOCK = 512
WINDOW = 2 * BLOCK
PIECE = 256
PIECES = WINDOW // PIECE
SUB = 128
CHUNKS = 4
NEAR, FAR = (1, 7, 2, 6), (3, 5, 4)
Z_ORDER = (4, 3, 5, 2, 6, 1, 7)
WHOLE, FRONT, BACK = slice(0, BLOCK), slice(0, BLOCK // 2), slice(BLOCK // 2, BLOCK)
Y_SLOT = (2, 0, 3, 4, 1, 5)
Y_SEM = (2, 0, 2, 2, 1, 2)
PARTS = 4


def split(x):
    high = x.astype(BF16)
    return high, (x - high.astype(F32)).astype(BF16)


def mm(a, b):
    return jnp.dot(a, b, preferred_element_type=F32)


def mm_exact(a, b):
    high, low = split(a)
    return mm(high, b) + mm(low, b)


def mm_split(a, b):
    a_high, a_low = split(a)
    b_high, b_low = split(b)
    return mm(a_high, b_high) + (mm(a_low, b_high) + mm(a_high, b_low))


def stacked(a, b):
    rows = a.shape[0]
    both = mm(jnp.concatenate(split(a), axis=0), b)
    return both[:rows] + both[rows:]


def within(size):
    row = lax.broadcasted_iota(jnp.int32, (SUB, SUB), 0)
    col = lax.broadcasted_iota(jnp.int32, (SUB, SUB), 1)
    return (row // (2 * size) == col // (2 * size)) & (row // size == col // size + 1)


def unit_inverse(block):
    row = lax.broadcasted_iota(jnp.int32, (SUB, SUB), 0)
    col = lax.broadcasted_iota(jnp.int32, (SUB, SUB), 1)
    inverse = jnp.where(row == col, 1.0, 0.0) - jnp.where(within(1), block, 0.0)
    size = 2
    while size < SUB // 2:
        below = jnp.where(within(size), block, 0.0).astype(BF16)
        inverse = inverse - mm_split(mm_exact(inverse, below), inverse)
        size *= 2
    return inverse


def kernel(
    a_hbm, b_hbm, rhs_hbm, panel_hbm, out_ref,
    a_v, b_v, bt, rhs_v, place, ut, yrecv, w, zrecv, g, lf, dall, mh, ml,
    load_b, load_a, load_s, y_s, y_r, z_s, z_r, gz_s, gz_r, gy_s, gy_r, px_s, px_r, pc_s, pc_r,
):
    row, col = lax.axis_index("row"), lax.axis_index("col")
    y, z = row // NZ, row % NZ
    x, core = col // 2, col % 2
    other = x * 2 + (1 - core)
    right = lax.rem(y + 1, NY) * NZ + z
    left = lax.rem(y + NY - 1, NY) * NZ + z
    depth, width = b_hbm.shape
    group = width // NY
    half = group // 2
    own = width // (NY * NZ)
    slab = panel_hbm.shape[1]

    def remote(src, dst, send, recv, r, c):
        return pltpu.make_async_remote_copy(
            src_ref=src, dst_ref=dst, send_sem=send, recv_sem=recv,
            device_id=(r, c), device_id_type=MESH,
        )

    def z_peer(d):
        return y * NZ + lax.rem(z + d, NZ)

    def y_peer(d):
        return lax.rem(y + d, NY) * NZ + z

    def z_rows(start, d):
        return pl.ds(pl.multiple_of(start + lax.rem(z + d, NZ) * own, own), own)

    def all_sent(sem, ref):
        remote(ref, ref, sem, sem, row, col).wait_send()

    def all_here(sem, ref):
        remote(ref, ref, sem, sem, row, col).wait_recv()

    def x_peer(d):
        return lax.rem(x + d, NX) * 2 + core

    barrier = pltpu.get_barrier_semaphore()

    def greet(r, c):
        pl.semaphore_signal(barrier, inc=1, device_id=(r, c), device_id_type=MESH)

    for d in Z_ORDER:
        greet(z_peer(d), col)
    for d in (2, 1, 3):
        greet(row, x_peer(d))
    for d in range(1, NY):
        greet(y_peer(d), col)
    greet(row, other)

    chunk = depth // CHUNKS
    load_panel = pltpu.make_async_copy(panel_hbm, lf.at[:, col], load_s.at[0])
    load_rhs = pltpu.make_async_copy(rhs_hbm, rhs_v, load_s.at[1])
    loads_b = [
        pltpu.make_async_copy(
            b_hbm.at[chunk * k : chunk * (k + 1), :], b_v.at[chunk * k : chunk * (k + 1), :], load_b.at[k]
        )
        for k in range(CHUNKS)
    ]

    def load(n):
        return pltpu.make_async_copy(a_hbm.at[:, PIECE * n : PIECE * (n + 1)], a_v.at[n], load_a.at[n])

    load_rhs.start()
    for copy in loads_b:
        copy.start()
    load(3).start()
    load_panel.start()

    for k in range(CHUNKS):
        loads_b[k].wait()
        bt[:, chunk * k : chunk * (k + 1)] = b_v[chunk * k : chunk * (k + 1), :].T

    load(2).start()


    def part(p, c):
        return dall.at[c] if p == 0 else lf.at[(1, 0, 2)[p - 1], c]

    def along_x(p, d):
        return remote(part(p, col), part(p, col), px_s.at[p], px_r.at[p, d - 1], row, x_peer(d))

    def across(p, d):
        shard = part(p, lax.rem(x + NX - d, NX) * 2 + core)
        return remote(shard, shard, pc_s.at[p], pc_r.at[p], row, other)

    def send_panel(p):
        for d in (2, 1, 3):
            along_x(p, d).start()
        across(p, 0).start()

    place[...] = jnp.zeros_like(place)
    load_rhs.wait()
    place[pl.ds(pl.multiple_of(z * (PIECE // NZ), 8), PIECE // NZ), :] = rhs_v[...]

    def y_group(target):
        return pl.multiple_of(target // NZ * group, group)

    right_rows, left_rows = y_group(right), y_group(left)
    far_rows = pl.multiple_of(lax.rem(y + 2, NY) * group, group)
    own_rows = pl.multiple_of(y * group, group)

    def y_copy(n, slot):
        start = ((right_rows, 1), (far_rows, 0), (right_rows, 0), (left_rows, 0), (far_rows, 1), (left_rows, 1))[slot]
        src = ut.at[n, pl.ds(start[0] + start[1] * half, half), :]
        target = right if slot < 3 else left
        return remote(src, yrecv.at[n, Y_SLOT[slot]], y_s, y_r.at[n, Y_SEM[slot]], target, col)

    def y_start(n, slots):
        for slot in slots:
            y_copy(n, slot).start()

    def update(n):
        load(n).wait()
        if n >= 2:
            load(n - 2).start()
        ut[n] = mm(bt[...], a_v[n])

        @pl.when(n == y)
        def _():
            ut[n] = ut[n] - place[...].T

    def relay(n):
        all_here(y_r.at[n, 0], yrecv.at[n, 0])
        ut[n, pl.ds(right_rows, half), :] += yrecv[n, 0]
        y_copy(n, 2).start()
        all_here(y_r.at[n, 1], yrecv.at[n, 1])
        ut[n, pl.ds(left_rows + half, half), :] += yrecv[n, 1]
        y_copy(n, 5).start()

    def z_copy(n, d):
        return remote(w.at[n, z_rows(0, d), :], zrecv.at[n, d - 1], z_s, z_r.at[n], z_peer(d), col)

    def y_sum(n):
        all_here(y_r.at[n, 2], yrecv.at[n, 2:6])
        w[n, :half, :] = ut[n, pl.ds(own_rows, half), :] + (yrecv[n, 3] + yrecv[n, 4])
        w[n, half:, :] = ut[n, pl.ds(own_rows + half, half), :] + (yrecv[n, 2] + yrecv[n, 5])
        for d in Z_ORDER:
            z_copy(n, d).start()

    def forward(p):
        for d in range(1, NX):
            along_x(p, d).wait_recv()
            across(p, d).start()

    def arrived(p):
        all_here(pc_r.at[p], dall.at[0:NX] if p == 0 else lf.at[0, 0:NX])

    update(3)
    pl.semaphore_wait(barrier, (NY - 1) + (NZ - 1) + (NX - 1) + 1)
    y_start(3, (1, 4))
    load_panel.wait()
    send_panel(1)
    update(2)
    y_start(2, (1, 4))
    y_start(3, (0, 3))
    update(1)
    y_start(1, (1, 4))
    at = pl.multiple_of(x * SUB, SUB)
    tiles = [lf[m, col, :, pl.ds(at, SUB)].astype(F32) for m in (0, 1)]
    turned = [pltpu.roll(tile, slab, 1) for tile in tiles]
    even = core == 0
    block = jnp.concatenate([jnp.where(even, tiles[0], turned[0]), jnp.where(even, turned[1], tiles[1])], axis=0)
    inverse = unit_inverse(block)
    dall[col] = inverse[:slab] + inverse[slab:]
    send_panel(0)
    relay(3)
    y_start(2, (0, 3))
    update(0)
    y_start(0, (1, 4))
    relay(2)
    y_start(1, (0, 3))
    relay(1)
    y_start(0, (0, 3))
    send_panel(2)
    forward(1)
    y_sum(3)
    relay(0)
    forward(0)
    send_panel(3)
    y_sum(2)
    y_sum(1)

    def whole_inverse(m):
        lane = lax.broadcasted_iota(jnp.int32, (slab, SUB), 1)

        def small(i):
            first, second = dall[2 * i], dall[2 * i + 1]
            if m == 0:
                second = pltpu.roll(second, slab, 1)
            else:
                first = pltpu.roll(first, slab, 1)
            first = jnp.where(lane < slab, first, 0.0)
            second = jnp.where(lane < slab, 0.0, second)
            value = jnp.concatenate([first, second], axis=0)
            diagonal = lower(i, i)
            below = jnp.where(within(slab), diagonal, jnp.zeros_like(diagonal))
            return value - mm_split(mm_exact(value, below), value)

        def lower(i, j):
            return lf[m, 2 * i : 2 * i + 2, :, SUB * j : SUB * (j + 1)].reshape(SUB, SUB)

        def pair(i):
            first, second = small(i), small(i + 1)
            below = -mm_split(mm_exact(second, lower(i + 1, i)), first)
            top = jnp.concatenate([first, jnp.zeros_like(first)], axis=1)
            return jnp.concatenate([top, jnp.concatenate([below, second], axis=1)], axis=0)

        first, second = pair(0), pair(2)
        off = lf[m, 4:, :, : 2 * SUB].reshape(2 * SUB, 2 * SUB)
        below = -mm_split(mm_exact(second, off), first)
        for rows, columns, value in (
            (slice(0, 2 * SUB), slice(0, 2 * SUB), first),
            (slice(0, 2 * SUB), slice(2 * SUB, BLOCK), jnp.zeros_like(first)),
            (slice(2 * SUB, BLOCK), slice(0, 2 * SUB), below),
            (slice(2 * SUB, BLOCK), slice(2 * SUB, BLOCK), second),
        ):
            high, low = split(value)
            mh[m, rows, columns] = high
            ml[m, rows, columns] = low

    def reduced(h):
        pieces = []
        for n in (2 * h, 2 * h + 1):
            all_here(z_r.at[n], zrecv.at[n])
            total = w[n, z_rows(0, 0), :]
            for d in range(1, NZ):
                total = total + zrecv[n, d - 1]
            pieces.append(-total)
        return jnp.concatenate(pieces, axis=1)

    def solve(h, value):
        return stacked(value, mh[h]) + mm(value.astype(BF16), ml[h])

    def gz_copy(h, d):
        rows = g.at[h, z_rows(own_rows, 0), :]
        return remote(rows, rows, gz_s, gz_r.at[h, 0 if d in NEAR else 1], z_peer(d), col)

    def gy_copy(h, d, start, columns, sem, side):
        rows = g.at[h, z_rows(start, d), columns]
        return remote(rows, rows, gy_s, gy_r.at[h, sem], y_peer(side), col)

    def spread(h, distances, wave):
        for d in distances:
            gy_copy(h, d, own_rows, WHOLE, wave, 1).start()
            gy_copy(h, d, own_rows, WHOLE, 3 + wave, 3).start()

    def pass_on(h, distances, wave):
        size = g.at[h, 0 : len(distances) * own, :]
        all_here(gy_r.at[h, wave], size)
        for d in distances:
            gy_copy(h, d, left_rows, FRONT, 6, 1).start()
        all_here(gy_r.at[h, 3 + wave], size)
        for d in distances:
            gy_copy(h, d, right_rows, BACK, 6, 3).start()

    def publish(h, value):
        g[h, z_rows(own_rows, 0), :] = value
        for d in Z_ORDER:
            gz_copy(h, d).start()
        spread(h, (0,), 0)

    def spread_near(h):
        all_here(gz_r.at[h, 0], g.at[h, 0 : 4 * own, :])
        spread(h, NEAR, 1)

    def spread_far(h):
        all_here(gz_r.at[h, 1], g.at[h, 0 : 3 * own, :])
        if h == 0:
            for d in FAR:
                gy_copy(h, d, own_rows, WHOLE, 6, 2).start()
        spread(h, FAR, 2)

    def finish(h):
        if h == 0:
            all_here(gy_r.at[h, 2], g.at[h, 0 : 3 * own, :])
            all_here(gy_r.at[h, 5], g.at[h, 0 : 3 * own, :])
        all_here(gy_r.at[h, 6], g.at[h, 0:group, :])
        out_ref[h * BLOCK : (h + 1) * BLOCK, :] = g[h].T

    arrived(0)
    arrived(1)
    whole_inverse(1)
    y_sum(0)
    forward(2)
    second = solve(1, reduced(1))
    publish(1, second)
    forward(3)
    arrived(2)
    whole_inverse(0)
    arrived(3)
    coupled = stacked(second, lf[2].reshape(BLOCK, BLOCK))
    first = solve(0, reduced(0) - coupled)
    publish(0, first)
    pass_on(1, (0,), 0)
    spread_near(1)
    spread_far(1)
    spread_near(0)
    pass_on(1, NEAR, 1)
    pass_on(0, (0,), 0)
    spread_far(0)
    pass_on(1, FAR, 2)
    all_sent(y_s, yrecv)
    all_sent(z_s, zrecv)
    for p in range(PARTS):
        across_size = dall.at[0:NX] if p == 0 else lf.at[0, 0:NX]
        along_size = dall.at[0 : NX - 1] if p == 0 else lf.at[0, 0 : NX - 1]
        all_sent(px_s.at[p], along_size)
        all_sent(pc_s.at[p], across_size)
    pass_on(0, NEAR, 1)
    finish(1)
    all_sent(gz_s, g.at[:, 0 : 7 * own, :])
    finish(0)
    all_sent(gy_s, g.at[:, 0 : 3 * group, :])


def shards(tail_factor, tail_solution, panel_rhs, panel_factor):
    depth, window = tail_factor.shape
    width = tail_solution.shape[1]
    group, own = width // NY, width // (NY * NZ)
    slab = panel_factor.shape[1]
    dma = pltpu.SemaphoreType.DMA
    scratch = [
        pltpu.VMEM((PIECES, depth, PIECE), BF16),
        pltpu.VMEM((depth, width), BF16),
        pltpu.VMEM((width, depth), BF16),
        pltpu.VMEM(panel_rhs.shape, F32),
        pltpu.VMEM((PIECE, width), F32),
        pltpu.VMEM((PIECES, width, PIECE), F32),
        pltpu.VMEM((PIECES, 6, group // 2, PIECE), F32),
        pltpu.VMEM((PIECES, group, PIECE), F32),
        pltpu.VMEM((PIECES, NZ - 1, own, PIECE), F32),
        pltpu.VMEM((2, width, BLOCK), F32),
        pltpu.VMEM((3, 2 * NX, slab, BLOCK), BF16),
        pltpu.VMEM((2 * NX, slab, SUB), F32),
        pltpu.VMEM((2, BLOCK, BLOCK), BF16),
        pltpu.VMEM((2, BLOCK, BLOCK), BF16),
        dma((CHUNKS,)), dma((PIECES,)), dma((2,)),
        dma, dma((PIECES, 3)),
        dma, dma((PIECES,)),
        dma, dma((2, 2)),
        dma, dma((2, 7)),
        dma((PARTS,)), dma((PARTS, NX - 1)),
        dma((PARTS,)), dma((PARTS,)),
    ]
    return pl.pallas_call(
        kernel,
        out_shape=jax.ShapeDtypeStruct((window, width), F32),
        in_specs=[pl.BlockSpec(memory_space=pltpu.HBM)] * 4,
        out_specs=pl.BlockSpec(memory_space=pltpu.VMEM),
        scratch_shapes=scratch,
        compiler_params=pltpu.CompilerParams(
            collective_id=0, has_side_effects=True, vmem_limit_bytes=52 * 1024 * 1024
        ),
    )(tail_factor, tail_solution, pltpu.with_memory_space_constraint(panel_rhs, pltpu.HBM), pltpu.with_memory_space_constraint(panel_factor, pltpu.HBM))


def solution(mesh):
    return jax.shard_map(
        shards,
        mesh=mesh,
        in_specs=(P("row", None), P("row", "col"), P("row", "col"), P(None, "col", None)),
        out_specs=P(None, "col"),
        check_vma=False,
    )
```
